32 devices in a mesh: section: 4 (over x, core), tp: 8 (over z, y).
Axes of the slice: x: 2, y: 2, z: 4, core: 2. Of those that a mesh axis runs over, the one named last changes fastest.
Arguments:
- layer_inputs: bfloat16 [8, 512, 4096], P('section', None, 'tp'), may hold values from -6 to 6
- weights: bfloat16 [8, 4096, 4096], P('section', 'tp'), may hold values from -0.046875 to 0.046875
- input_basis: bfloat16 [8, 4096, 64], P('section', 'tp'), may hold values from -0.09375 to 0.09375
- output_basis: bfloat16 [8, 4096, 32], P('section', 'tp'), may hold values from -0.09375 to 0.09375
- queries: bfloat16 [8, 512, 2048], P('section', 'tp'), may hold values from -0.00390625 to 0.00390625
- top_cotangent: bfloat16 [512, 4096], replicated, may hold values from -6 to 6
- sequence_example: int32 [4], replicated, may hold values from 0 to 1
Outputs:
- scores: float32 [2, 512], P(None, 'tp')
The draws below stay inside these ranges and needn't reach their ends.
All inputs are finite; a program needn't handle non-finite values.
Results may differ from the reference program's by a relative error of at most 0.0094.
Values may be sent and summed in bfloat16 or wider, within the bound.
A program may use at most 64 MiB of HBM per device.

```python
import jax
import jax.numpy as jnp
from jax import lax

D = 4096
RIN = 64
ROUT = 32
NQ = 512
SEQLEN = 128
LAYERS = 8
KDIM = 2048
SEQS = 4
TOKENS = 512
EXAMPLES = 2


def set_ends(values, stream_key, low, high):
    shape = values.shape
    spot = [jax.random.randint(jax.random.fold_in(stream_key, axis), (), 0, shape[axis]) for axis in range(len(shape))]
    values = values.at[tuple(spot)].set(low)
    longest = shape.index(max(shape))
    spot[longest] = (spot[longest] + 1) % shape[longest]
    return values.at[tuple(spot)].set(high)


def block_scale(own_key, extent, split, least, top_value):
    def one(axis_at, parts):
        steps = jax.random.uniform(jax.random.fold_in(jax.random.fold_in(own_key, 6), axis_at), (parts,), jnp.float32, least / len(split), top_value / len(split))
        return jnp.repeat(jnp.exp(steps), extent[axis_at] // parts).reshape((-1,) + (1,) * (len(extent) - axis_at - 1))

    factor_of = one(*split[0])
    for cut in split[1:]:
        factor_of = factor_of * one(*cut)
    return factor_of


def scatter_about(key, shape, deviation, most, pieces=(), kind=jnp.bfloat16):
    drawn = jax.random.normal(key, shape, jnp.float32) * deviation
    if len(pieces) > 0:
        drawn = block_scale(key, shape, pieces, -0.22, 0.18) * drawn
    return jnp.clip(drawn, min=-most, max=most).astype(kind)


def setup_inputs(seed: int = 0) -> dict:
    streams_of = jax.random.split(jax.random.key(seed), 8)
    layer_inputs = scatter_about(streams_of[0], (LAYERS, TOKENS, D), 1.0, 6.0, ((0, 4), (2, 8)))
    weights = scatter_about(streams_of[1], (LAYERS, D, D), (4 * D) ** -0.5, 0.046875, ((0, 4), (1, 8)))
    input_basis = scatter_about(streams_of[2], (LAYERS, D, RIN), D ** -0.5, 0.09375, ((0, 4), (1, 8)))
    output_basis = scatter_about(streams_of[3], (LAYERS, D, ROUT), D ** -0.5, 0.09375, ((0, 4), (1, 8)))
    queries = scatter_about(streams_of[4], (LAYERS, NQ, KDIM), (KDIM * 1024) ** -0.5, 0.00390625, ((0, 4), (1, 8)))
    top_cotangent = scatter_about(streams_of[5], (TOKENS, D), 1.0, 6.0)
    sequence_example = set_ends(jax.random.randint(streams_of[6], (SEQS,), 0, EXAMPLES), jax.random.fold_in(streams_of[6], 1), 0, EXAMPLES - 1).astype(jnp.int32)
    return dict(layer_inputs=layer_inputs, weights=weights, input_basis=input_basis, output_basis=output_basis, queries=queries, top_cotangent=top_cotangent, sequence_example=sequence_example)


def reference(layer_inputs, weights, input_basis, output_basis, queries, top_cotangent, sequence_example):
    token_examples = jnp.repeat(sequence_example, SEQLEN)
    selector = (jnp.arange(EXAMPLES, dtype=jnp.int32)[:, None] == token_examples[None, :]).astype(jnp.float32)

    def layer_step(cotangent, inputs):
        hidden, matrix, basis_in, basis_out, stored_queries = inputs
        floats = hidden.astype(jnp.float32)
        logistic = jax.nn.sigmoid(floats)
        activated = (floats * logistic).astype(jnp.bfloat16)
        slope = logistic * (1.0 + floats * (1.0 - logistic))
        in_feats = jnp.dot(activated, basis_in, preferred_element_type=jnp.float32)
        out_feats = jnp.dot(cotangent, basis_out, preferred_element_type=jnp.float32)
        joined = (out_feats[:, :, None] * in_feats[:, None, :]).reshape(out_feats.shape[0], -1)
        grads = jnp.dot(selector, joined, precision=lax.Precision.HIGHEST)
        layer_scores = jnp.dot(grads, stored_queries.astype(jnp.float32).T, precision=lax.Precision.HIGHEST)
        branch = jnp.dot(cotangent, matrix.T, preferred_element_type=jnp.float32)
        updated = (cotangent.astype(jnp.float32) + slope * branch).astype(jnp.bfloat16)
        return updated, layer_scores

    final, stacked = lax.scan(layer_step, top_cotangent, (layer_inputs, weights, input_basis, output_basis, queries), reverse=True)
    return jnp.sum(stacked, axis=0)
```

```python
import functools

import jax
import jax.numpy as jnp
from jax import lax
from jax.experimental import pallas as pl
from jax.experimental.pallas import tpu as pltpu
from jax.sharding import PartitionSpec as P

EXAMPLES = 2
ROWS = 32
MESH = pl.DeviceIdType.MESH
NT = (((1,), (1,)), ((), ()))


def grid_of(tp_count):
    ny = 1
    while (2 * ny) * (2 * ny) <= tp_count:
        ny *= 2
    return tp_count // ny, ny


def slope_of(hidden):
    floats = hidden.astype(jnp.float32)
    logistic = jax.nn.sigmoid(floats)
    return logistic * (1.0 + floats * (1.0 - logistic))


def chain_kernel(
    sections, tp_count, top_ref, w_ref, h_ref, ib_ref, ob_ref, q_ref, se_ref, score_ref,
    buf_u, buf_m, buf_l, w_v, ob_v, ib_v, out_v, part_in, got_in, full_in, grad_v, sum_v, score_v,
    w_sem, recv_u, recv_m, send_m, send_u, send_my, relay_u, relay_m, send_l, send_ly,
    part_send, part_recv, full_send, full_recv, grad_send, grad_recv, score_send, score_recv,
):
    nz, ny = grid_of(tp_count)
    sec = lax.axis_index("section")
    tp = lax.axis_index("tp")
    z, y = tp // ny, lax.rem(tp, ny)
    micro, _, rows, width = buf_u.shape
    is_top = sec == sections - 1
    has_lower = sec > 0
    pair_lower = lax.rem(sec, 2) == 1
    pair_upper = jnp.logical_not(pair_lower)
    far_fed = jnp.logical_and(pair_lower, jnp.logical_not(is_top))

    far = [z]
    for k in range(nz - 1):
        down = nz - 1 - k
        from_low = down - (z >= down).astype(jnp.int32)
        from_high = k + (z <= k).astype(jnp.int32)
        far.append(jnp.where(z < nz // 2, from_low, from_high))
    near = far[:1] + far[:0:-1]

    def peer_z(step):
        return far[step] * ny + y

    def peer_y(step):
        return z * ny + lax.rem(y + step, ny)

    def src_at(zstep, ystep):
        return near[zstep] * ny + lax.rem(y + ystep, ny)

    def w_copy(layer):
        return pltpu.make_async_copy(w_ref.at[layer], w_v.at[layer], w_sem.at[layer])

    def top_copy(m, k):
        return pltpu.make_async_copy(
            top_ref.at[pl.ds(pl.multiple_of(m * rows, rows), rows), pl.ds(k * width, width)],
            buf_u.at[m, k], recv_u.at[m, k])

    def remote(src, dst, ssem, rsem, to_sec, to_tp):
        return pltpu.make_async_remote_copy(
            src_ref=src, dst_ref=dst, send_sem=ssem, recv_sem=rsem,
            device_id=(to_sec, to_tp), device_id_type=MESH)

    rank_in, rank_out = ib_ref.shape[1], ob_ref.shape[1]

    def prepare_bases():
        gap_in = jnp.zeros((rank_in, width), jnp.float32)
        gap_out = jnp.zeros((EXAMPLES * rank_out, width), jnp.float32)
        for layer in range(2):
            basis_in = ib_ref[layer].astype(jnp.float32)
            basis_out = [ob_ref[layer].astype(jnp.float32)] * EXAMPLES
            ins = [basis_in, gap_in] if layer == 0 else [gap_in, basis_in]
            outs = basis_out + [gap_out] if layer == 0 else [gap_out] + basis_out
            ib_v[layer] = jnp.concatenate(ins, 0).astype(jnp.bfloat16)
            ob_v[layer] = jnp.concatenate(outs, 0).astype(jnp.bfloat16)

    @pl.when(is_top)
    def _():
        @pl.loop(0, micro)
        def _(m):
            for k in range(tp_count):
                top_copy(m, k).start()

    w_copy(1).start()

    @pl.when(has_lower)
    def _():
        w_copy(0).start()

    barrier = pltpu.get_barrier_semaphore()

    def greet(to_sec, to_tp):
        pl.semaphore_signal(barrier, inc=1, device_id=(to_sec, to_tp), device_id_type=MESH)

    for step in range(1, tp_count):
        greet(sec, lax.rem(tp + step, tp_count))

    partner = sec + 1 - 2 * lax.rem(sec, 2)
    for step in range(1, nz):
        greet(partner, peer_z(step))
    for step in range(1, ny):
        greet(partner, peer_y(step))
    for step in range(1, sections):
        greet(lax.rem(sec + step, sections), tp)

    prepare_bases()
    pl.semaphore_wait(barrier, tp_count + nz + ny + sections - 4)

    def relay_u_copy(m, zstep, ystep):
        src = src_at(zstep, 0)
        return remote(buf_u.at[m, src], buf_u.at[m, src], relay_u.at[m, zstep, ystep],
                      recv_u.at[m, src], sec, peer_y(ystep))

    def relay_m_copy(m, zstep, ystep):
        src = src_at(zstep, 0)
        return remote(buf_m.at[m, src], buf_m.at[m, src], relay_m.at[m, zstep, ystep],
                      recv_m.at[m, src], sec, peer_y(ystep))

    def middle_copy(m, zstep):
        return remote(buf_m.at[m, tp], buf_m.at[m, tp], send_m.at[m, zstep],
                      recv_m.at[m, tp], sec, peer_z(zstep))

    def upper_copy(m, zstep):
        return remote(buf_u.at[m, tp], buf_u.at[m, tp], send_u.at[m, zstep],
                      recv_u.at[m, tp], sec, peer_z(zstep))

    def lower_copy(m, zstep):
        return remote(buf_l.at[m], buf_u.at[m, tp], send_l.at[m, zstep],
                      recv_u.at[m, tp], sec - 1, peer_z(zstep))

    def lower_y_copy(m, ystep):
        return remote(buf_l.at[m], buf_u.at[m, tp], send_ly.at[m, ystep],
                      recv_u.at[m, tp], sec - 1, peer_y(ystep))

    def await_u(m, src):
        remote(buf_u.at[m, src], buf_u.at[m, src], send_my, recv_u.at[m, src], sec, tp).wait_recv()

    def await_m(m, src):
        remote(buf_m.at[m, src], buf_m.at[m, src], send_my, recv_m.at[m, src], sec, tp).wait_recv()

    def product(buf, m, layer, ystep, total=None):
        for zstep in range(nz):
            src = src_at(zstep, ystep)
            columns = pl.ds(pl.multiple_of(src * width, width), width)
            term = lax.dot_general(
                buf[m, src], w_v[layer, :, columns], NT, preferred_element_type=jnp.float32)
            total = term if total is None else total + term
        return total

    def upper(m):
        at = pl.ds(pl.multiple_of(m * rows, rows), rows)
        own = buf_u[m, tp]
        floats = own.astype(jnp.float32)
        slope = slope_of(h_ref[1, at, :])
        total = product(buf_u, m, 1, 0)
        for ystep in range(1, ny):
            @pl.when(jnp.logical_not(is_top))
            def _(ystep=ystep):
                for zstep in range(nz):
                    await_u(m, src_at(zstep, ystep))

            total = product(buf_u, m, 1, ystep, total)
        middle = (floats + slope * total).astype(jnp.bfloat16)
        buf_m[m, tp] = middle

        @pl.when(has_lower)
        def _():
            for step in range(1, nz):
                middle_copy(m, step).start()
            for step in range(1, ny):
                relay_m_copy(m, 0, step).start()

        feats = lax.dot_general(
            own, ob_v[1], NT, preferred_element_type=jnp.float32
        ) + lax.dot_general(middle, ob_v[0], NT, preferred_element_type=jnp.float32)
        example = se_ref[m * rows // (micro * rows // se_ref.shape[0])]
        lane_example = lax.rem(
            lax.broadcasted_iota(jnp.int32, feats.shape, 1) // rank_out, EXAMPLES)
        out_v[at, :] = jnp.where(lane_example == example, feats, 0.0)

    def lower(m):
        at = pl.ds(pl.multiple_of(m * rows, rows), rows)
        floats = buf_m[m, tp].astype(jnp.float32)
        slope = slope_of(h_ref[0, at, :])
        total = product(buf_m, m, 0, 0)
        for ystep in range(1, ny):
            for zstep in range(nz):
                await_m(m, src_at(zstep, ystep))
            total = product(buf_m, m, 0, ystep, total)
        buf_l[m] = (floats + slope * total).astype(jnp.bfloat16)

        @pl.when(pair_lower)
        def _():
            for step in range(1, nz):
                lower_copy(m, step).start()
            for step in range(1, ny):
                lower_y_copy(m, step).start()

        lower_copy(m, 0).start()

    def tp_copy(src, dst, ssem, rsem, to_tp):
        return remote(src, dst, ssem, rsem, sec, to_tp)

    def part_copy(step):
        to = lax.rem(tp + step, tp_count)
        return tp_copy(part_in.at[to], got_in.at[tp], part_send.at[step], part_recv.at[tp], to)

    def full_copy(step):
        to = lax.rem(tp + step, tp_count)
        return tp_copy(full_in.at[tp], full_in.at[tp], full_send.at[step], full_recv.at[tp], to)

    def grad_copy(step):
        to = lax.rem(tp + step, tp_count)
        return tp_copy(grad_v.at[tp], grad_v.at[tp], grad_send.at[step], grad_recv.at[tp], to)

    def score_copy(step):
        to = lax.rem(sec + step, sections)
        return remote(score_v.at[sec], score_v.at[sec], score_send.at[step],
                      score_recv.at[sec], to, tp)

    def project_inputs():
        part_rows = part_in.shape[1]

        @pl.loop(0, tp_count)
        def _(k):
            at = pl.ds(pl.multiple_of(k * part_rows, part_rows), part_rows)
            total = None
            for layer in range(2):
                floats = h_ref[layer, at, :].astype(jnp.float32)
                activated = (floats * jax.nn.sigmoid(floats)).astype(jnp.bfloat16)
                term = lax.dot_general(
                    activated, ib_v[layer], NT, preferred_element_type=jnp.float32)
                total = term if total is None else total + term
            part_in[k] = total

        for step in range(1, tp_count):
            part_copy(step).start()
        total = part_in[tp]
        for step in range(1, tp_count):
            src = lax.rem(tp + step, tp_count)
            tp_copy(got_in.at[src], got_in.at[src], send_my, part_recv.at[src], tp).wait_recv()
            total = total + got_in[src]
        full_in[tp] = total
        for step in range(1, tp_count):
            full_copy(step).start()

    @pl.when(sec < sections // 2)
    def _():
        project_inputs()

    def spread_upper(m):
        await_u(m, tp)
        for step in range(1, nz):
            upper_copy(m, step).start()
        for step in range(1, ny):
            relay_u_copy(m, 0, step).start()

    def pass_upper(m):
        @pl.when(pair_upper)
        def _():
            await_u(m, tp)

        for zstep in range(1, nz):
            await_u(m, src_at(zstep, 0))
            for ystep in range(1, ny):
                relay_u_copy(m, zstep, ystep).start()

    def pass_middle(m):
        for zstep in range(1, nz):
            await_m(m, src_at(zstep, 0))
            for ystep in range(1, ny):
                relay_m_copy(m, zstep, ystep).start()

    def within(m):
        return jnp.logical_and(m >= 0, m < micro)

    lag_pass = far_fed.astype(jnp.int32)
    lag_upper = jnp.where(is_top, 0, lag_pass + 1)

    @pl.loop(0, micro + 5)
    def _(it):
        m_pass = it - lag_pass
        m_up = it - lag_upper
        m_mid = m_up - 1
        m_low = m_up - 2

        @pl.when(jnp.logical_and(it < micro, far_fed))
        def _():
            spread_upper(it)

        @pl.when(jnp.logical_and(within(m_pass), jnp.logical_not(is_top)))
        def _():
            pass_upper(m_pass)

        @pl.when(m_up == 0)
        def _():
            w_copy(1).wait()

        @pl.when(within(m_up))
        def _():
            @pl.when(is_top)
            def _():
                for k in range(tp_count):
                    top_copy(m_up, k).wait()

            upper(m_up)

        @pl.when(jnp.logical_and(within(m_mid), has_lower))
        def _():
            pass_middle(m_mid)

        @pl.when(jnp.logical_and(m_low == 0, has_lower))
        def _():
            w_copy(0).wait()

        @pl.when(jnp.logical_and(within(m_low), has_lower))
        def _():
            lower(m_low)

    @pl.when(sec >= sections // 2)
    def _():
        project_inputs()

    for step in range(1, tp_count):
        src = lax.rem(tp + step, tp_count)
        tp_copy(full_in.at[src], full_in.at[src], send_my, full_recv.at[src], tp).wait_recv()
    lanes = 2 * rank_in
    pairs = EXAMPLES * rank_out
    product_all = lax.dot_general(
        out_v[...], full_in[...].reshape(micro * rows, lanes), (((0,), (0,)), ((), ())),
        precision=lax.Precision.HIGHEST, preferred_element_type=jnp.float32)
    lane = lax.broadcasted_iota(jnp.int32, (pairs, lanes), 1)
    grad_v[tp] = jnp.where(lane < rank_in, product_all[:pairs], product_all[pairs:])
    for step in range(1, tp_count):
        grad_copy(step).start()
    for step in range(1, tp_count):
        src = lax.rem(tp + step, tp_count)
        tp_copy(grad_v.at[src], grad_v.at[src], send_my, grad_recv.at[src], tp).wait_recv()
    total = grad_v[0]
    for k in range(1, tp_count):
        total = total + grad_v[k]
    sum_v[...] = total
    half = rank_out // 2
    number = q_ref.shape[1]
    sums = []
    for example in range(EXAMPLES):
        even = sum_v[pl.ds(example * rank_out, half, stride=2), :]
        odd = sum_v[pl.ds(example * rank_out + 1, half, stride=2), :]
        acc = jnp.zeros((number, lanes), jnp.float32)
        for layer in range(2):
            part = slice(layer * rank_in, (layer + 1) * rank_in)
            tiles = jnp.concatenate([even[:, part], odd[:, part]], 1)
            for j in range(half):
                block = q_ref[layer, :, j * lanes:(j + 1) * lanes].astype(jnp.float32)
                acc = acc + tiles[j:j + 1, :] * block
        sums.append(acc)
    score_v[sec] = lax.dot_general(
        jnp.ones((8, lanes), jnp.float32), jnp.concatenate(sums, 0), NT,
        precision=lax.Precision.HIGHEST, preferred_element_type=jnp.float32)
    for step in range(1, sections):
        score_copy(step).start()
    for step in range(1, sections):
        src = lax.rem(sec + step, sections)
        remote(score_v.at[src], score_v.at[src], send_my, score_recv.at[src], sec, tp).wait_recv()
    total = score_v[0]
    for k in range(1, sections):
        total = total + score_v[k]
    for example in range(EXAMPLES):
        score_ref[example:example + 1, :] = total[0:1, example * number:(example + 1) * number]

    for step in range(1, tp_count):
        part_copy(step).wait_send()
        full_copy(step).wait_send()
        grad_copy(step).wait_send()
    for step in range(1, sections):
        score_copy(step).wait_send()

    @pl.loop(0, micro)
    def _(m):
        @pl.when(far_fed)
        def _():
            for zstep in range(1, nz):
                upper_copy(m, zstep).wait_send()
            for ystep in range(1, ny):
                relay_u_copy(m, 0, ystep).wait_send()

        @pl.when(jnp.logical_not(is_top))
        def _():
            for zstep in range(1, nz):
                for ystep in range(1, ny):
                    relay_u_copy(m, zstep, ystep).wait_send()

        @pl.when(has_lower)
        def _():
            for zstep in range(1, nz):
                middle_copy(m, zstep).wait_send()
            for zstep in range(nz):
                for ystep in range(1, ny):
                    relay_m_copy(m, zstep, ystep).wait_send()
            lower_copy(m, 0).wait_send()

        @pl.when(pair_lower)
        def _():
            for zstep in range(1, nz):
                lower_copy(m, zstep).wait_send()
            for ystep in range(1, ny):
                lower_y_copy(m, ystep).wait_send()


def shards(
    layer_inputs, weights, input_basis, output_basis, queries, top_cotangent, sequence_example
):
    sections = lax.axis_size("section")
    tp_count = lax.axis_size("tp")
    tokens, width = layer_inputs.shape[1:]
    rows = ROWS
    micro = tokens // rows
    nz, ny = grid_of(tp_count)
    lanes = 2 * input_basis.shape[2]
    pairs = EXAMPLES * output_basis.shape[2]
    number = queries.shape[1]
    dma = pltpu.SemaphoreType.DMA
    vmem = pl.BlockSpec(memory_space=pltpu.VMEM)
    hbm = pl.BlockSpec(memory_space=pl.ANY)
    smem = pl.BlockSpec(memory_space=pltpu.SMEM)
    return pl.pallas_call(
        functools.partial(chain_kernel, sections, tp_count),
        out_shape=jax.ShapeDtypeStruct((EXAMPLES, number), jnp.float32),
        in_specs=[hbm, hbm, vmem, vmem, vmem, vmem, smem],
        out_specs=vmem,
        scratch_shapes=[
            pltpu.VMEM((micro, tp_count, rows, width), jnp.bfloat16),
            pltpu.VMEM((micro, tp_count, rows, width), jnp.bfloat16),
            pltpu.VMEM((micro, rows, width), jnp.bfloat16),
            pltpu.VMEM(weights.shape, jnp.bfloat16),
            pltpu.VMEM((2, 2 * pairs, width), jnp.bfloat16),
            pltpu.VMEM((2, lanes, width), jnp.bfloat16),
            pltpu.VMEM((tokens, 2 * pairs), jnp.float32),
            pltpu.VMEM((tp_count, tokens // tp_count, lanes), jnp.float32),
            pltpu.VMEM((tp_count, tokens // tp_count, lanes), jnp.float32),
            pltpu.VMEM((tp_count, tokens // tp_count, lanes), jnp.float32),
            pltpu.VMEM((tp_count, pairs, lanes), jnp.float32),
            pltpu.VMEM((pairs, lanes), jnp.float32),
            pltpu.VMEM((sections, 8, EXAMPLES * number), jnp.float32),
            dma((2,)),
            dma((micro, tp_count)),
            dma((micro, tp_count)),
            dma((micro, nz)),
            dma((micro, nz)),
            dma,
            dma((micro, nz, ny)),
            dma((micro, nz, ny)),
            dma((micro, nz)),
            dma((micro, ny)),
            dma((tp_count,)),
            dma((tp_count,)),
            dma((tp_count,)),
            dma((tp_count,)),
            dma((tp_count,)),
            dma((tp_count,)),
            dma((sections,)),
            dma((sections,)),
        ],
        compiler_params=pltpu.CompilerParams(
            collective_id=0, has_side_effects=True, vmem_limit_bytes=56 * 2**20),
    )(
        top_cotangent, weights, layer_inputs, jnp.swapaxes(input_basis, 1, 2),
        jnp.swapaxes(output_basis, 1, 2), queries, sequence_example)


def solution(mesh):
    placed = (
        P("section", None, "tp"),
        P("section", "tp", None),
        P("section", "tp", None),
        P("section", "tp", None),
        P("section", "tp", None),
        P(),
        P(),
    )
    return jax.shard_map(
        shards, mesh=mesh, in_specs=placed, out_specs=P(None, "tp"), check_vma=False
    )
```

```python
import functools

import jax
import jax.numpy as jnp
from jax import lax
from jax.experimental import pallas as pl
from jax.experimental.pallas import tpu as pltpu
from jax.sharding import PartitionSpec as P

EXAMPLES = 2
ROWS = 32
TOP_ROUTED = (0, 0)
LOW_ROUTED = (0, 0)
LAGS = ((0, 0, 1, 2), (0, 1, 2, 3), (1, 2, 3, 4), (0, 1, 1, 1))
MESH = pl.DeviceIdType.MESH
NT = (((1,), (1,)), ((), ()))
NN = (((1,), (0,)), ((), ()))


def grid_of(tp_count):
    ny = 1
    while (2 * ny) * (2 * ny) <= tp_count:
        ny *= 2
    return tp_count // ny, ny


def slope_of(hidden):
    floats = hidden.astype(jnp.float32)
    logistic = jax.nn.sigmoid(floats)
    return logistic * (1.0 + floats * (1.0 - logistic))


def chain_kernel(
    sections, tp_count, top_ref, w_ref, h_ref, ib_ref, ob_ref, q_ref, se_ref, score_ref,
    buf_u, buf_m, buf_l, buf_v, w_v, w_t, ob_v, ib_v, out_v, part_in, got_in, full_in, grad_v, sum_v, score_v,
    w_sem, top_sem, recv_x, recv_u, recv_m, near_u, near_m, recv_v, send_u, send_m, send_l, send_v, send_my,
    part_send, part_recv, full_send, full_recv, grad_send, grad_recv, score_send, score_recv,
):
    nz, ny = grid_of(tp_count)
    sec = lax.axis_index("section")
    tp = lax.axis_index("tp")
    z, y = tp // ny, lax.rem(tp, ny)
    micro, _, rows, width = buf_u.shape
    is_top = sec == sections - 1
    has_lower = sec > 0
    pair_lower = lax.rem(sec, 2) == 1
    pair_upper = jnp.logical_not(pair_lower)
    relays = sorted({(sections - 1, sections - 4), (3, 0)}) if sections >= 4 else []

    def in_span(m, span):
        return jnp.logical_and(m >= span[0], m < span[1])

    def top_routed(m):
        return in_span(m, TOP_ROUTED if relays else (0, 0))

    def low_routed(m):
        return in_span(m, LOW_ROUTED if relays else (0, 0))

    far_fed = jnp.logical_and(pair_lower, jnp.logical_not(is_top))

    far = [z]
    for k in range(nz - 1):
        down = nz - 1 - k
        from_low = down - (z >= down).astype(jnp.int32)
        from_high = k + (z <= k).astype(jnp.int32)
        far.append(jnp.where(z < nz // 2, from_low, from_high))
    near = far[:1] + far[:0:-1]
    mate = z + 1 - 2 * lax.rem(z, 2)

    def peer_z(step):
        return far[step] * ny + y

    def peer_y(step):
        return z * ny + lax.rem(y + step, ny)

    def src_at(zstep, ystep):
        return near[zstep] * ny + lax.rem(y + ystep, ny)

    def w_copy(layer):
        return pltpu.make_async_copy(w_ref.at[layer], w_v.at[layer], w_sem.at[layer])

    def top_copy(m, k):
        return pltpu.make_async_copy(
            top_ref.at[pl.ds(pl.multiple_of(m * rows, rows), rows), pl.ds(k * width, width)],
            buf_u.at[m, k], top_sem.at[m])

    def remote(src, dst, ssem, rsem, to_sec, to_tp):
        return pltpu.make_async_remote_copy(
            src_ref=src, dst_ref=dst, send_sem=ssem, recv_sem=rsem,
            device_id=(to_sec, to_tp), device_id_type=MESH)

    rank_in, rank_out = ib_ref.shape[1], ob_ref.shape[1]

    def prepare_bases():
        gap_in = jnp.zeros((rank_in, width), jnp.float32)
        gap_out = jnp.zeros((EXAMPLES * rank_out, width), jnp.float32)
        for layer in range(2):
            basis_in = ib_ref[layer].astype(jnp.float32)
            basis_out = [ob_ref[layer].astype(jnp.float32)] * EXAMPLES
            ins = [basis_in, gap_in] if layer == 0 else [gap_in, basis_in]
            outs = basis_out + [gap_out] if layer == 0 else [gap_out] + basis_out
            ib_v[layer] = jnp.concatenate(ins, 0).astype(jnp.bfloat16)
            ob_v[layer] = jnp.concatenate(outs, 0).astype(jnp.bfloat16)

    @pl.when(is_top)
    def _():
        @pl.loop(0, micro)
        def _(m):
            for k in range(tp_count):
                top_copy(m, k).start()

    w_copy(1).start()

    @pl.when(has_lower)
    def _():
        w_copy(0).start()

    barrier = pltpu.get_barrier_semaphore()

    def greet(to_sec, to_tp):
        pl.semaphore_signal(barrier, inc=1, device_id=(to_sec, to_tp), device_id_type=MESH)

    for step in range(1, tp_count):
        greet(sec, lax.rem(tp + step, tp_count))

    partner = sec + 1 - 2 * lax.rem(sec, 2)
    for step in range(1, nz):
        greet(partner, peer_z(step))
    for step in range(1, ny):
        greet(partner, peer_y(step))
    for step in range(1, sections):
        greet(lax.rem(sec + step, sections), tp)
    linked = 0
    for pair in relays:
        for here, there in (pair, pair[::-1]):
            @pl.when(sec == here)
            def _(there=there):
                for step in range(1, tp_count):
                    greet(there, lax.rem(tp + step, tp_count))

            linked = linked + (sec == here).astype(jnp.int32)

    def turn_weights(layer):
        w_copy(layer).wait()

        @pl.loop(0, tp_count)
        def _(k):
            columns = pl.ds(pl.multiple_of(k * width, width), width)
            w_t[layer, columns, :] = w_v[layer, :, columns].T

    prepare_bases()
    turn_weights(1)

    @pl.when(jnp.logical_and(has_lower, jnp.logical_not(is_top)))
    def _():
        turn_weights(0)

    pl.semaphore_wait(barrier, tp_count + nz + ny + sections - 4 + (tp_count - 1) * linked)

    def slots(buf, m, count, ssem, rsem):
        part = buf.at[m, pl.ds(0, count)]
        return remote(part, part, ssem, rsem, sec, tp)

    def relay_copy(buf, sends, recvs, m, zstep, ystep):
        src = src_at(zstep, 0)
        return remote(buf.at[m, src], buf.at[m, src], sends.at[m],
                      recvs.at[m, ny - ystep], sec, peer_y(ystep))

    def forward_copy(buf, sends, recvs, m, ystep):
        src = src_at(0, ystep)
        return remote(buf.at[m, src], buf.at[m, src], sends.at[m],
                      recvs.at[m, ystep], sec, mate * ny + y)

    def spread_copy(buf, sends, recvs, m, zstep):
        return remote(buf.at[m, tp], buf.at[m, tp], sends.at[m], recvs.at[m, 0], sec, peer_z(zstep))

    def lower_own_copy(m):
        return remote(buf_l.at[m], buf_u.at[m, tp], send_l.at[m], recv_x.at[m], sec - 1, tp)

    def lower_z_copy(m, zstep):
        return remote(buf_l.at[m], buf_u.at[m, tp], send_l.at[m], recv_u.at[m, 0],
                      sec - 1, peer_z(zstep))

    def lower_y_copy(m, ystep):
        return remote(buf_l.at[m], buf_u.at[m, tp], send_l.at[m], near_u.at[m, ny - ystep],
                      sec - 1, peer_y(ystep))

    def await_own(m):
        remote(buf_u.at[m, tp], buf_u.at[m, tp], send_my, recv_x.at[m], sec, tp).wait_recv()

    def await_line(buf, recvs, m, ystep):
        slots(buf, m, nz - 1, send_my, recvs.at[m, ystep]).wait_recv()

    def await_near(buf, nears, m, ystep):
        slots(buf, m, 1, send_my, nears.at[m, ystep]).wait_recv()

    def pass_on(buf, sends, recvs, nears, m):
        for ystep in range(1, ny):
            await_near(buf, nears, m, ystep)
            forward_copy(buf, sends, recvs, m, ystep).start()
        await_line(buf, recvs, m, 0)
        for zstep in range(2, nz):
            for ystep in range(1, ny):
                relay_copy(buf, sends, recvs, m, zstep, ystep).start()

    def routed_on(buf, recvs, nears, m, target):
        remote(buf_v.at[m], buf_v.at[m], send_my, recv_v.at[m], sec, tp).wait_recv()
        for zstep in [*range(nz - 1, 0, -1), 0]:
            for ystep in range(ny):
                if zstep or ystep:
                    sem = recvs if zstep else nears
                    remote(buf_v.at[m], buf.at[m, tp], send_v.at[m], sem.at[m, (ny - ystep) % ny],
                           target, src_at(zstep, ystep)).start()

    def product(buf, m, layer, ystep, total=None):
        for zstep in range(nz):
            src = src_at(zstep, ystep)
            columns = pl.ds(pl.multiple_of(src * width, width), width)
            term = lax.dot_general(
                buf[m, src], w_t[layer, columns, :], NN, preferred_element_type=jnp.float32)
            total = term if total is None else total + term
        return total

    def upper(m):
        at = pl.ds(pl.multiple_of(m * rows, rows), rows)
        own = buf_u[m, tp]
        floats = own.astype(jnp.float32)
        slope = slope_of(h_ref[1, at, :])

        @pl.when(jnp.logical_and(sec == 0, low_routed(m)))
        def _():
            await_line(buf_u, recv_u, m, 0)
            for ystep in range(1, ny):
                await_near(buf_u, near_u, m, ystep)

        total = product(buf_u, m, 1, 0)
        for ystep in range(1, ny):
            @pl.when(jnp.logical_not(is_top))
            def _(ystep=ystep):
                await_line(buf_u, recv_u, m, ystep)

            total = product(buf_u, m, 1, ystep, total)
        middle = (floats + slope * total).astype(jnp.bfloat16)
        buf_m[m, tp] = middle

        routed = jnp.logical_and(is_top, top_routed(m))

        @pl.when(jnp.logical_and(has_lower, jnp.logical_not(routed)))
        def _():
            for step in range(1, nz):
                spread_copy(buf_m, send_m, recv_m, m, step).start()
            for step in range(1, ny):
                relay_copy(buf_m, send_m, near_m, m, 0, step).start()

        if relays:
            @pl.when(routed)
            def _():
                remote(buf_m.at[m, tp], buf_v.at[m], send_m.at[m], recv_v.at[m],
                       sections - 4, tp).start()

        feats = lax.dot_general(
            own, ob_v[1], NT, preferred_element_type=jnp.float32
        ) + lax.dot_general(middle, ob_v[0], NT, preferred_element_type=jnp.float32)
        example = se_ref[m * rows // (micro * rows // se_ref.shape[0])]
        lane_example = lax.rem(
            lax.broadcasted_iota(jnp.int32, feats.shape, 1) // rank_out, EXAMPLES)
        out_v[at, :] = jnp.where(lane_example == example, feats, 0.0)

    def lower(m):
        at = pl.ds(pl.multiple_of(m * rows, rows), rows)
        floats = buf_m[m, tp].astype(jnp.float32)
        slope = slope_of(h_ref[0, at, :])

        @pl.when(jnp.logical_and(is_top, top_routed(m)))
        def _():
            await_line(buf_m, recv_m, m, 0)
            for ystep in range(1, ny):
                await_near(buf_m, near_m, m, ystep)

        total = product(buf_m, m, 0, 0)
        for ystep in range(1, ny):
            await_line(buf_m, recv_m, m, ystep)
            total = product(buf_m, m, 0, ystep, total)
        buf_l[m] = (floats + slope * total).astype(jnp.bfloat16)

        routed = jnp.logical_and(sec == 1, low_routed(m))

        @pl.when(jnp.logical_and(pair_lower, jnp.logical_not(routed)))
        def _():
            for step in range(1, nz):
                lower_z_copy(m, step).start()
            for step in range(1, ny):
                lower_y_copy(m, step).start()

        if relays:
            @pl.when(routed)
            def _():
                remote(buf_l.at[m], buf_v.at[m], send_l.at[m], recv_v.at[m], 3, tp).start()

        lower_own_copy(m).start()

    def tp_copy(src, dst, ssem, rsem, to_tp):
        return remote(src, dst, ssem, rsem, sec, to_tp)

    def part_copy(step):
        to = lax.rem(tp + step, tp_count)
        return tp_copy(part_in.at[to], got_in.at[tp], part_send.at[step], part_recv.at[tp], to)

    def full_copy(step):
        to = lax.rem(tp + step, tp_count)
        return tp_copy(full_in.at[tp], full_in.at[tp], full_send.at[step], full_recv.at[tp], to)

    def grad_copy(step):
        to = lax.rem(tp + step, tp_count)
        return tp_copy(grad_v.at[tp], grad_v.at[tp], grad_send.at[step], grad_recv.at[tp], to)

    def score_copy(step):
        to = lax.rem(sec + step, sections)
        return remote(score_v.at[sec], score_v.at[sec], score_send.at[step],
                      score_recv.at[sec], to, tp)

    def project_inputs():
        part_rows = part_in.shape[1]

        @pl.loop(0, tp_count)
        def _(k):
            at = pl.ds(pl.multiple_of(k * part_rows, part_rows), part_rows)
            total = None
            for layer in range(2):
                floats = h_ref[layer, at, :].astype(jnp.float32)
                activated = (floats * jax.nn.sigmoid(floats)).astype(jnp.bfloat16)
                term = lax.dot_general(
                    activated, ib_v[layer], NT, preferred_element_type=jnp.float32)
                total = term if total is None else total + term
            part_in[k] = total

        for step in range(1, tp_count):
            part_copy(step).start()
        total = part_in[tp]
        for step in range(1, tp_count):
            src = lax.rem(tp + step, tp_count)
            tp_copy(got_in.at[src], got_in.at[src], send_my, part_recv.at[src], tp).wait_recv()
            total = total + got_in[src]
        full_in[tp] = total
        for step in range(1, tp_count):
            full_copy(step).start()

    @pl.when(sec < sections // 2)
    def _():
        project_inputs()

    def spread_upper(m):
        await_own(m)
        for step in range(1, nz):
            spread_copy(buf_u, send_u, recv_u, m, step).start()
        for step in range(1, ny):
            relay_copy(buf_u, send_u, near_u, m, 0, step).start()

    def pass_upper(m):
        @pl.when(pair_upper)
        def _():
            await_own(m)

        @pl.when(jnp.logical_not(jnp.logical_and(sec == 0, low_routed(m))))
        def _():
            pass_on(buf_u, send_u, recv_u, near_u, m)

    def pass_middle(m):
        @pl.when(jnp.logical_not(jnp.logical_and(is_top, top_routed(m))))
        def _():
            pass_on(buf_m, send_m, recv_m, near_m, m)

    def within(m):
        return jnp.logical_and(m >= 0, m < micro)

    kind = jnp.where(is_top, 0, jnp.where(far_fed, 2, jnp.where(has_lower, 1, 3)))

    def lag_of(k):
        lag = LAGS[0][k]
        for other in range(1, 4):
            lag = jnp.where(kind == other, LAGS[other][k], lag)
        return lag

    lag_pass, lag_upper, lag_middle, lag_lower = [lag_of(k) for k in range(4)]
    steps = micro + max(max(lags) for lags in LAGS)

    if relays:
        @pl.when(sec == sections - 4)
        def _():
            @pl.loop(*TOP_ROUTED)
            def _(m):
                routed_on(buf_m, recv_m, near_m, m, sections - 1)

    @pl.loop(0, steps)
    def _(it):
        m_pass = it - lag_pass
        m_up = it - lag_upper
        m_mid = it - lag_middle
        m_low = it - lag_lower

        @pl.when(jnp.logical_and(it < micro, far_fed))
        def _():
            spread_upper(it)

        @pl.when(jnp.logical_and(within(m_pass), jnp.logical_not(is_top)))
        def _():
            pass_upper(m_pass)

        @pl.when(within(m_up))
        def _():
            @pl.when(is_top)
            def _():
                pltpu.make_async_copy(
                    buf_u.at[m_up], buf_u.at[m_up], top_sem.at[m_up]).wait()

            upper(m_up)

        @pl.when(jnp.logical_and(it == 0, is_top))
        def _():
            turn_weights(0)

        @pl.when(jnp.logical_and(within(m_mid), has_lower))
        def _():
            pass_middle(m_mid)

        @pl.when(jnp.logical_and(within(m_low), has_lower))
        def _():
            lower(m_low)

    @pl.when(sec >= sections // 2)
    def _():
        project_inputs()

    if relays:
        @pl.when(sec == 3)
        def _():
            @pl.loop(*LOW_ROUTED)
            def _(m):
                routed_on(buf_u, recv_u, near_u, m, 0)

    for step in range(1, tp_count):
        src = lax.rem(tp + step, tp_count)
        tp_copy(full_in.at[src], full_in.at[src], send_my, full_recv.at[src], tp).wait_recv()
    lanes = 2 * rank_in
    pairs = EXAMPLES * rank_out
    product_all = lax.dot_general(
        out_v[...], full_in[...].reshape(micro * rows, lanes), (((0,), (0,)), ((), ())),
        precision=lax.Precision.HIGHEST, preferred_element_type=jnp.float32)
    lane = lax.broadcasted_iota(jnp.int32, (pairs, lanes), 1)
    own_grad = jnp.where(lane < rank_in, product_all[:pairs], product_all[pairs:])
    grad_v[tp] = own_grad.astype(jnp.bfloat16)
    for step in range(1, tp_count):
        grad_copy(step).start()
    for step in range(1, tp_count):
        src = lax.rem(tp + step, tp_count)
        tp_copy(grad_v.at[src], grad_v.at[src], send_my, grad_recv.at[src], tp).wait_recv()
    total = grad_v[0].astype(jnp.float32)
    for k in range(1, tp_count):
        total = total + grad_v[k].astype(jnp.float32)
    sum_v[...] = total
    half = rank_out // 2
    number = q_ref.shape[1]
    sums = []
    for example in range(EXAMPLES):
        even = sum_v[pl.ds(example * rank_out, half, stride=2), :]
        odd = sum_v[pl.ds(example * rank_out + 1, half, stride=2), :]
        acc = jnp.zeros((number, lanes), jnp.float32)
        for layer in range(2):
            part = slice(layer * rank_in, (layer + 1) * rank_in)
            tiles = jnp.concatenate([even[:, part], odd[:, part]], 1)
            for j in range(half):
                block = q_ref[layer, :, j * lanes:(j + 1) * lanes].astype(jnp.float32)
                acc = acc + tiles[j:j + 1, :] * block
        sums.append(acc)
    score_v[sec] = lax.dot_general(
        jnp.ones((8, lanes), jnp.float32), jnp.concatenate(sums, 0), NT,
        precision=lax.Precision.HIGHEST, preferred_element_type=jnp.float32)
    for step in range(1, sections):
        score_copy(step).start()
    for step in range(1, sections):
        src = lax.rem(sec + step, sections)
        remote(score_v.at[src], score_v.at[src], send_my, score_recv.at[src], sec, tp).wait_recv()
    total = score_v[0]
    for k in range(1, sections):
        total = total + score_v[k]
    for example in range(EXAMPLES):
        score_ref[example:example + 1, :] = total[0:1, example * number:(example + 1) * number]

    for step in range(1, tp_count):
        part_copy(step).wait_send()
        full_copy(step).wait_send()
        grad_copy(step).wait_send()
    for step in range(1, sections):
        score_copy(step).wait_send()

    def sent(sends, buf, m, count, when):
        @pl.when(when)
        def _():
            slots(buf, m, count, sends.at[m], send_my).wait_send()

    @pl.loop(0, micro)
    def _(m):
        top_far = jnp.logical_and(is_top, top_routed(m))
        low_far = jnp.logical_and(sec == 1, low_routed(m))
        in_far = jnp.logical_and(sec == 0, low_routed(m))
        sent(send_u, buf_u, m, tp_count - 1, far_fed)
        sent(send_u, buf_u, m, (nz - 1) * (ny - 1),
             jnp.logical_and(jnp.logical_and(pair_upper, ny > 1), jnp.logical_not(in_far)))
        sent(send_m, buf_m, m, tp_count - 1, jnp.logical_and(has_lower, jnp.logical_not(top_far)))
        sent(send_m, buf_m, m, 1, top_far)
        sent(send_l, buf_u, m, nz + ny - 1, jnp.logical_and(pair_lower, jnp.logical_not(low_far)))
        sent(send_l, buf_u, m, 2, low_far)
        sent(send_l, buf_u, m, 1, jnp.logical_and(pair_upper, has_lower))
        if relays:
            sent(send_v, buf_u, m, tp_count - 1, jnp.logical_or(
                jnp.logical_and(sec == sections - 4, top_routed(m)),
                jnp.logical_and(sec == 3, low_routed(m))))


def shards(
    layer_inputs, weights, input_basis, output_basis, queries, top_cotangent, sequence_example
):
    sections = lax.axis_size("section")
    tp_count = lax.axis_size("tp")
    tokens, width = layer_inputs.shape[1:]
    rows = ROWS
    micro = tokens // rows
    nz, ny = grid_of(tp_count)
    lanes = 2 * input_basis.shape[2]
    pairs = EXAMPLES * output_basis.shape[2]
    number = queries.shape[1]
    dma = pltpu.SemaphoreType.DMA
    vmem = pl.BlockSpec(memory_space=pltpu.VMEM)
    hbm = pl.BlockSpec(memory_space=pl.ANY)
    smem = pl.BlockSpec(memory_space=pltpu.SMEM)
    return pl.pallas_call(
        functools.partial(chain_kernel, sections, tp_count),
        out_shape=jax.ShapeDtypeStruct((EXAMPLES, number), jnp.float32),
        in_specs=[hbm, hbm, vmem, vmem, vmem, vmem, smem],
        out_specs=vmem,
        scratch_shapes=[
            pltpu.VMEM((micro, tp_count, rows, width), jnp.bfloat16),
            pltpu.VMEM((micro, tp_count, rows, width), jnp.bfloat16),
            pltpu.VMEM((micro, rows, width), jnp.bfloat16),
            pltpu.VMEM((micro, rows, width), jnp.bfloat16),
            pltpu.VMEM(weights.shape, jnp.bfloat16),
            pltpu.VMEM((2, weights.shape[2], width), jnp.bfloat16),
            pltpu.VMEM((2, 2 * pairs, width), jnp.bfloat16),
            pltpu.VMEM((2, lanes, width), jnp.bfloat16),
            pltpu.VMEM((tokens, 2 * pairs), jnp.float32),
            pltpu.VMEM((tp_count, tokens // tp_count, lanes), jnp.float32),
            pltpu.VMEM((tp_count, tokens // tp_count, lanes), jnp.float32),
            pltpu.VMEM((tp_count, tokens // tp_count, lanes), jnp.float32),
            pltpu.VMEM((tp_count, pairs, lanes), jnp.bfloat16),
            pltpu.VMEM((pairs, lanes), jnp.float32),
            pltpu.VMEM((sections, 8, EXAMPLES * number), jnp.float32),
            dma((2,)),
            dma((micro,)),
            dma((micro,)),
            dma((micro, ny)),
            dma((micro, ny)),
            dma((micro, ny)),
            dma((micro, ny)),
            dma((micro,)),
            dma((micro,)),
            dma((micro,)),
            dma((micro,)),
            dma((micro,)),
            dma,
            dma((tp_count,)),
            dma((tp_count,)),
            dma((tp_count,)),
            dma((tp_count,)),
            dma((tp_count,)),
            dma((tp_count,)),
            dma((sections,)),
            dma((sections,)),
        ],
        compiler_params=pltpu.CompilerParams(
            collective_id=0, has_side_effects=True, vmem_limit_bytes=56 * 2**20),
    )(
        top_cotangent, weights, layer_inputs, jnp.swapaxes(input_basis, 1, 2),
        jnp.swapaxes(output_basis, 1, 2), queries, sequence_example)


def solution(mesh):
    placed = (
        P("section", None, "tp"),
        P("section", "tp", None),
        P("section", "tp", None),
        P("section", "tp", None),
        P("section", "tp", None),
        P(),
        P(),
    )
    return jax.shard_map(
        shards, mesh=mesh, in_specs=placed, out_specs=P(None, "tp"), check_vma=False
    )
```

```python
import functools

import jax
import jax.numpy as jnp
from jax import lax
from jax.experimental import pallas as pl
from jax.experimental.pallas import tpu as pltpu
from jax.sharding import PartitionSpec as P

EXAMPLES = 2
ROWS = 32
TOP_ROUTED = (4, 11)
DIRECT = (11, 16)
LAGS = ((0, 0, 2, 3), (0, 1, 2, 3), (1, 2, 3, 4), (0, 1, 1, 1))
MESH = pl.DeviceIdType.MESH
NT = (((1,), (1,)), ((), ()))
NN = (((1,), (0,)), ((), ()))


def grid_of(tp_count):
    ny = 1
    while (2 * ny) * (2 * ny) <= tp_count:
        ny *= 2
    return tp_count // ny, ny


def slope_of(hidden):
    floats = hidden.astype(jnp.float32)
    logistic = jax.nn.sigmoid(floats)
    return logistic * (1.0 + floats * (1.0 - logistic))


def chain_kernel(
    sections, tp_count, top_ref, w_ref, h_ref, ib_ref, ob_ref, q_ref, se_ref, score_ref,
    buf_u, buf_m, buf_l, buf_v, w_v, w_t, ob_v, ib_v, out_v, part_in, got_in, full_in, grad_v, sum_v, score_v,
    w_sem, top_sem, recv_x, recv_u, recv_m, near_u, near_m, recv_v, send_u, send_m, send_l, send_v, send_my,
    part_send, part_recv, full_send, full_recv, grad_send, grad_recv, score_send, score_recv,
):
    nz, ny = grid_of(tp_count)
    sec = lax.axis_index("section")
    tp = lax.axis_index("tp")
    z, y = tp // ny, lax.rem(tp, ny)
    micro, _, rows, width = buf_u.shape
    is_top = sec == sections - 1
    has_lower = sec > 0
    pair_lower = lax.rem(sec, 2) == 1
    pair_upper = jnp.logical_not(pair_lower)
    helper = sections - 4

    def scaled(span):
        return [part * micro // 16 for part in span]

    def in_span(m, span):
        low, high = scaled(span)
        return jnp.logical_and(m >= low, m < high)

    def top_routed(m):
        return in_span(m, TOP_ROUTED if helper >= 0 else (0, 0))

    def direct(m):
        return in_span(m, DIRECT)

    far_fed = jnp.logical_and(pair_lower, jnp.logical_not(is_top))
    far_lower = jnp.logical_and(pair_upper, has_lower)

    far = [z]
    for k in range(nz - 1):
        down = nz - 1 - k
        from_low = down - (z >= down).astype(jnp.int32)
        from_high = k + (z <= k).astype(jnp.int32)
        far.append(jnp.where(z < nz // 2, from_low, from_high))
    near = far[:1] + far[:0:-1]
    mate = z + 1 - 2 * lax.rem(z, 2)

    def peer_z(step):
        return far[step] * ny + y

    def peer_y(step):
        return z * ny + lax.rem(y + step, ny)

    def src_at(zstep, ystep):
        return near[zstep] * ny + lax.rem(y + ystep, ny)

    def w_copy(layer):
        return pltpu.make_async_copy(w_ref.at[layer], w_v.at[layer], w_sem.at[layer])

    def top_copy(m, k):
        return pltpu.make_async_copy(
            top_ref.at[pl.ds(pl.multiple_of(m * rows, rows), rows), pl.ds(k * width, width)],
            buf_u.at[m, k], top_sem.at[m])

    def remote(src, dst, ssem, rsem, to_sec, to_tp):
        return pltpu.make_async_remote_copy(
            src_ref=src, dst_ref=dst, send_sem=ssem, recv_sem=rsem,
            device_id=(to_sec, to_tp), device_id_type=MESH)

    rank_in, rank_out = ib_ref.shape[1], ob_ref.shape[1]

    def prepare_bases():
        gap_in = jnp.zeros((rank_in, width), jnp.float32)
        gap_out = jnp.zeros((EXAMPLES * rank_out, width), jnp.float32)
        for layer in range(2):
            basis_in = ib_ref[layer].astype(jnp.float32)
            basis_out = [ob_ref[layer].astype(jnp.float32)] * EXAMPLES
            ins = [basis_in, gap_in] if layer == 0 else [gap_in, basis_in]
            outs = basis_out + [gap_out] if layer == 0 else [gap_out] + basis_out
            ib_v[layer] = jnp.concatenate(ins, 0).astype(jnp.bfloat16)
            ob_v[layer] = jnp.concatenate(outs, 0).astype(jnp.bfloat16)

    @pl.when(is_top)
    def _():
        @pl.loop(0, micro)
        def _(m):
            for k in range(tp_count):
                top_copy(m, k).start()

    w_copy(1).start()

    @pl.when(has_lower)
    def _():
        w_copy(0).start()

    barrier = pltpu.get_barrier_semaphore()

    def greet(to_sec, to_tp):
        pl.semaphore_signal(barrier, inc=1, device_id=(to_sec, to_tp), device_id_type=MESH)

    for step in range(1, tp_count):
        greet(sec, lax.rem(tp + step, tp_count))

    partner = sec + 1 - 2 * lax.rem(sec, 2)
    for step in range(1, nz):
        greet(partner, peer_z(step))
    for step in range(1, ny):
        greet(partner, peer_y(step))
    for step in range(1, sections):
        greet(lax.rem(sec + step, sections), tp)
    linked = 0
    for when, there in ((far_fed, sec + 1), (far_lower, sec - 1)):
        @pl.when(when)
        def _(there=there):
            for step in range(1, nz):
                greet(there, peer_z(step))
            for step in range(1, ny):
                greet(there, peer_y(step))

        linked = linked + (nz + ny - 2) * when.astype(jnp.int32)
    if helper >= 0:
        for here, there in ((sections - 1, helper), (helper, sections - 1)):
            @pl.when(sec == here)
            def _(there=there):
                for step in range(1, tp_count):
                    greet(there, lax.rem(tp + step, tp_count))

            linked = linked + (tp_count - 1) * (sec == here).astype(jnp.int32)

    def turn_weights(layer):
        w_copy(layer).wait()

        @pl.loop(0, tp_count)
        def _(k):
            columns = pl.ds(pl.multiple_of(k * width, width), width)
            w_t[layer, columns, :] = w_v[layer, :, columns].T

    prepare_bases()
    turn_weights(1)

    @pl.when(jnp.logical_and(has_lower, jnp.logical_not(is_top)))
    def _():
        turn_weights(0)

    pl.semaphore_wait(barrier, tp_count + nz + ny + sections - 4 + linked)

    def slots(buf, m, count, ssem, rsem):
        part = buf.at[m, pl.ds(0, count)]
        return remote(part, part, ssem, rsem, sec, tp)

    def relay_copy(buf, sends, recvs, m, zstep, ystep):
        src = src_at(zstep, 0)
        line = ny - ystep - (0 if zstep else 1)
        return remote(buf.at[m, src], buf.at[m, src], sends.at[m],
                      recvs.at[m, line], sec, peer_y(ystep))

    def forward_copy(buf, sends, recvs, m, ystep):
        src = src_at(0, ystep)
        return remote(buf.at[m, src], buf.at[m, src], sends.at[m],
                      recvs.at[m, ystep], sec, mate * ny + y)

    def spread_copy(buf, sends, recvs, m, zstep):
        return remote(buf.at[m, tp], buf.at[m, tp], sends.at[m], recvs.at[m, 0], sec, peer_z(zstep))

    def lower_own_copy(m):
        return remote(buf_l.at[m], buf_u.at[m, tp], send_l.at[m], recv_x.at[m], sec - 1, tp)

    def lower_z_copy(m, zstep):
        return remote(buf_l.at[m], buf_u.at[m, tp], send_l.at[m], recv_u.at[m, 0],
                      sec - 1, peer_z(zstep))

    def lower_y_copy(m, ystep):
        return remote(buf_l.at[m], buf_u.at[m, tp], send_l.at[m], near_u.at[m, ny - ystep - 1],
                      sec - 1, peer_y(ystep))

    def await_own(m):
        remote(buf_u.at[m, tp], buf_u.at[m, tp], send_my, recv_x.at[m], sec, tp).wait_recv()

    def await_line(buf, recvs, m, ystep):
        slots(buf, m, nz - 1, send_my, recvs.at[m, ystep]).wait_recv()

    def await_near(buf, nears, m, ystep):
        slots(buf, m, 1, send_my, nears.at[m, ystep - 1]).wait_recv()

    def pass_on(buf, sends, recvs, nears, m):
        for ystep in range(1, ny):
            await_near(buf, nears, m, ystep)
            forward_copy(buf, sends, recvs, m, ystep).start()
        await_line(buf, recvs, m, 0)
        for zstep in range(2, nz):
            for ystep in range(1, ny):
                relay_copy(buf, sends, recvs, m, zstep, ystep).start()

    def routed_on(buf, recvs, nears, m, target):
        remote(buf_v.at[m], buf_v.at[m], send_my, recv_v.at[m], sec, tp).wait_recv()
        for zstep in [*range(nz - 1, 0, -1), 0]:
            for ystep in range(ny):
                if zstep or ystep:
                    line = (ny - ystep) % ny
                    sem = recvs.at[m, line] if zstep else nears.at[m, line - 1]
                    remote(buf_v.at[m], buf.at[m, tp], send_v.at[m], sem,
                           target, src_at(zstep, ystep)).start()

    def product(buf, m, layer, ystep, total=None):
        for zstep in range(nz):
            src = src_at(zstep, ystep)
            columns = pl.ds(pl.multiple_of(src * width, width), width)
            term = lax.dot_general(
                buf[m, src], w_t[layer, columns, :], NN, preferred_element_type=jnp.float32)
            total = term if total is None else total + term
        return total

    def upper(m):
        at = pl.ds(pl.multiple_of(m * rows, rows), rows)
        own = buf_u[m, tp]
        floats = own.astype(jnp.float32)
        slope = slope_of(h_ref[1, at, :])
        total = product(buf_u, m, 1, 0)
        for ystep in range(1, ny):
            @pl.when(jnp.logical_not(is_top))
            def _(ystep=ystep):
                await_line(buf_u, recv_u, m, ystep)

            total = product(buf_u, m, 1, ystep, total)
        middle = (floats + slope * total).astype(jnp.bfloat16)
        buf_m[m, tp] = middle

        routed = jnp.logical_and(is_top, top_routed(m))

        @pl.when(jnp.logical_and(has_lower, jnp.logical_not(routed)))
        def _():
            for step in range(1, nz):
                spread_copy(buf_m, send_m, recv_m, m, step).start()
            for step in range(1, ny):
                relay_copy(buf_m, send_m, near_m, m, 0, step).start()

        if helper >= 0:
            @pl.when(routed)
            def _():
                remote(buf_m.at[m, tp], buf_v.at[m], send_m.at[m], recv_v.at[m],
                       helper, tp).start()

        feats = lax.dot_general(
            own, ob_v[1], NT, preferred_element_type=jnp.float32
        ) + lax.dot_general(middle, ob_v[0], NT, preferred_element_type=jnp.float32)
        example = se_ref[m * rows // (micro * rows // se_ref.shape[0])]
        lane_example = lax.rem(
            lax.broadcasted_iota(jnp.int32, feats.shape, 1) // rank_out, EXAMPLES)
        out_v[at, :] = jnp.where(lane_example == example, feats, 0.0)

    def lower(m):
        at = pl.ds(pl.multiple_of(m * rows, rows), rows)
        floats = buf_m[m, tp].astype(jnp.float32)
        slope = slope_of(h_ref[0, at, :])

        @pl.when(jnp.logical_and(is_top, top_routed(m)))
        def _():
            await_line(buf_m, recv_m, m, 0)
            for ystep in range(1, ny):
                await_near(buf_m, near_m, m, ystep)

        total = product(buf_m, m, 0, 0)
        for ystep in range(1, ny):
            await_line(buf_m, recv_m, m, ystep)
            total = product(buf_m, m, 0, ystep, total)
        buf_l[m] = (floats + slope * total).astype(jnp.bfloat16)

        @pl.when(jnp.logical_or(pair_lower, direct(m)))
        def _():
            for step in range(1, nz):
                lower_z_copy(m, step).start()
            for step in range(1, ny):
                lower_y_copy(m, step).start()

        lower_own_copy(m).start()

    def tp_copy(src, dst, ssem, rsem, to_tp):
        return remote(src, dst, ssem, rsem, sec, to_tp)

    others = [(zstep, ystep) for zstep in [*range(nz - 1, 0, -1), 0]
              for ystep in range(ny) if zstep or ystep]

    def share(src_of, dst_ref, ssem, rsem):
        for zstep, ystep in others:
            to = src_at(zstep, ystep)
            tp_copy(src_of(to), dst_ref, ssem, rsem, to).start()

    def shared(buf, ssem, rsem):
        part = buf.at[pl.ds(0, tp_count - 1)]
        return tp_copy(part, part, ssem, rsem, tp)

    def score_copy(step):
        to = lax.rem(sec + step, sections)
        return remote(score_v.at[sec], score_v.at[sec], score_send,
                      score_recv, to, tp)

    def project_inputs():
        part_rows = part_in.shape[1]

        @pl.loop(0, tp_count)
        def _(k):
            at = pl.ds(pl.multiple_of(k * part_rows, part_rows), part_rows)
            total = None
            for layer in range(2):
                floats = h_ref[layer, at, :].astype(jnp.float32)
                activated = (floats * jax.nn.sigmoid(floats)).astype(jnp.bfloat16)
                term = lax.dot_general(
                    activated, ib_v[layer], NT, preferred_element_type=jnp.float32)
                total = term if total is None else total + term
            part_in[k] = total

        share(lambda to: part_in.at[to], got_in.at[tp], part_send, part_recv)
        total = part_in[tp]
        shared(got_in, send_my, part_recv).wait_recv()
        for step in range(1, tp_count):
            total = total + got_in[lax.rem(tp + step, tp_count)]
        full_in[tp] = total
        share(lambda to: full_in.at[tp], full_in.at[tp], full_send, full_recv)

    @pl.when(sec < sections // 2)
    def _():
        project_inputs()

    def spread_upper(m):
        await_own(m)
        for step in range(1, nz):
            spread_copy(buf_u, send_u, recv_u, m, step).start()
        for step in range(1, ny):
            relay_copy(buf_u, send_u, near_u, m, 0, step).start()

    def pass_upper(m):
        @pl.when(jnp.logical_or(pair_upper, direct(m)))
        def _():
            await_own(m)

        pass_on(buf_u, send_u, recv_u, near_u, m)

    def pass_middle(m):
        @pl.when(jnp.logical_not(jnp.logical_and(is_top, top_routed(m))))
        def _():
            pass_on(buf_m, send_m, recv_m, near_m, m)

    def within(m):
        return jnp.logical_and(m >= 0, m < micro)

    kind = jnp.where(is_top, 0, jnp.where(far_fed, 2, jnp.where(has_lower, 1, 3)))

    def lag_of(k):
        lag = LAGS[0][k]
        for other in range(1, 4):
            lag = jnp.where(kind == other, LAGS[other][k], lag)
        return lag

    lag_pass, lag_upper, lag_middle, lag_lower = [lag_of(k) for k in range(4)]
    steps = micro + max(max(lags) for lags in LAGS)

    if helper >= 0:
        @pl.when(sec == helper)
        def _():
            @pl.loop(*scaled(TOP_ROUTED))
            def _(m):
                routed_on(buf_m, recv_m, near_m, m, sections - 1)

    @pl.loop(0, steps)
    def _(it):
        m_pass = it - lag_pass
        m_up = it - lag_upper
        m_mid = it - lag_middle
        m_low = it - lag_lower

        @pl.when(jnp.logical_and(jnp.logical_and(it < micro, far_fed), jnp.logical_not(direct(it))))
        def _():
            spread_upper(it)

        @pl.when(jnp.logical_and(within(m_pass), jnp.logical_not(is_top)))
        def _():
            pass_upper(m_pass)

        @pl.when(within(m_up))
        def _():
            @pl.when(is_top)
            def _():
                pltpu.make_async_copy(
                    buf_u.at[m_up], buf_u.at[m_up], top_sem.at[m_up]).wait()

            upper(m_up)

        @pl.when(jnp.logical_and(it == 0, is_top))
        def _():
            turn_weights(0)

        @pl.when(jnp.logical_and(within(m_mid), has_lower))
        def _():
            pass_middle(m_mid)

        @pl.when(jnp.logical_and(within(m_low), has_lower))
        def _():
            lower(m_low)

    @pl.when(sec >= sections // 2)
    def _():
        project_inputs()

    shared(full_in, send_my, full_recv).wait_recv()
    lanes = 2 * rank_in
    pairs = EXAMPLES * rank_out
    product_all = lax.dot_general(
        out_v[...], full_in[...].reshape(micro * rows, lanes), (((0,), (0,)), ((), ())),
        precision=lax.Precision.HIGHEST, preferred_element_type=jnp.float32)
    lane = lax.broadcasted_iota(jnp.int32, (pairs, lanes), 1)
    own_grad = jnp.where(lane < rank_in, product_all[:pairs], product_all[pairs:])
    grad_v[tp] = own_grad.astype(jnp.bfloat16)
    share(lambda to: grad_v.at[tp], grad_v.at[tp], grad_send, grad_recv)
    shared(grad_v, send_my, grad_recv).wait_recv()
    total = grad_v[0].astype(jnp.float32)
    for k in range(1, tp_count):
        total = total + grad_v[k].astype(jnp.float32)
    sum_v[...] = total
    half = rank_out // 2
    number = q_ref.shape[1]
    sums = []
    for example in range(EXAMPLES):
        even = sum_v[pl.ds(example * rank_out, half, stride=2), :]
        odd = sum_v[pl.ds(example * rank_out + 1, half, stride=2), :]
        acc = jnp.zeros((number, lanes), jnp.float32)
        for layer in range(2):
            part = slice(layer * rank_in, (layer + 1) * rank_in)
            tiles = jnp.concatenate([even[:, part], odd[:, part]], 1)
            for j in range(half):
                block = q_ref[layer, :, j * lanes:(j + 1) * lanes].astype(jnp.float32)
                acc = acc + tiles[j:j + 1, :] * block
        sums.append(acc)
    score_v[sec] = lax.dot_general(
        jnp.ones((8, lanes), jnp.float32), jnp.concatenate(sums, 0), NT,
        precision=lax.Precision.HIGHEST, preferred_element_type=jnp.float32)
    for step in range(1, sections):
        score_copy(step).start()
    scores = score_v.at[pl.ds(0, sections - 1)]
    remote(scores, scores, send_my, score_recv, sec, tp).wait_recv()
    total = score_v[0]
    for k in range(1, sections):
        total = total + score_v[k]
    for example in range(EXAMPLES):
        score_ref[example:example + 1, :] = total[0:1, example * number:(example + 1) * number]

    shared(part_in, part_send, send_my).wait_send()
    shared(full_in, full_send, send_my).wait_send()
    shared(grad_v, grad_send, send_my).wait_send()
    remote(scores, scores, score_send, send_my, sec, tp).wait_send()

    def sent(sends, buf, m, count, when):
        @pl.when(when)
        def _():
            slots(buf, m, count, sends.at[m], send_my).wait_send()

    @pl.loop(0, micro)
    def _(m):
        top_far = jnp.logical_and(is_top, top_routed(m))
        spread = jnp.logical_and(far_fed, jnp.logical_not(direct(m)))
        hop = jnp.logical_and(far_lower, jnp.logical_not(direct(m)))
        sent(send_u, buf_u, m, tp_count - 1, spread)
        if ny > 1:
            sent(send_u, buf_u, m, (nz - 1) * (ny - 1),
                 jnp.logical_not(jnp.logical_or(is_top, spread)))
        sent(send_m, buf_m, m, tp_count - 1, jnp.logical_and(has_lower, jnp.logical_not(top_far)))
        sent(send_m, buf_m, m, 1, top_far)
        sent(send_l, buf_u, m, nz + ny - 1, jnp.logical_and(has_lower, jnp.logical_not(hop)))
        sent(send_l, buf_u, m, 1, hop)
        if helper >= 0:
            sent(send_v, buf_u, m, tp_count - 1,
                 jnp.logical_and(sec == helper, top_routed(m)))


def shards(
    layer_inputs, weights, input_basis, output_basis, queries, top_cotangent, sequence_example
):
    sections = lax.axis_size("section")
    tp_count = lax.axis_size("tp")
    tokens, width = layer_inputs.shape[1:]
    rows = ROWS
    micro = tokens // rows
    nz, ny = grid_of(tp_count)
    lanes = 2 * input_basis.shape[2]
    pairs = EXAMPLES * output_basis.shape[2]
    number = queries.shape[1]
    dma = pltpu.SemaphoreType.DMA
    vmem = pl.BlockSpec(memory_space=pltpu.VMEM)
    hbm = pl.BlockSpec(memory_space=pl.ANY)
    smem = pl.BlockSpec(memory_space=pltpu.SMEM)
    return pl.pallas_call(
        functools.partial(chain_kernel, sections, tp_count),
        out_shape=jax.ShapeDtypeStruct((EXAMPLES, number), jnp.float32),
        in_specs=[hbm, hbm, vmem, vmem, vmem, vmem, smem],
        out_specs=vmem,
        scratch_shapes=[
            pltpu.VMEM((micro, tp_count, rows, width), jnp.bfloat16),
            pltpu.VMEM((micro, tp_count, rows, width), jnp.bfloat16),
            pltpu.VMEM((micro, rows, width), jnp.bfloat16),
            pltpu.VMEM((micro, rows, width), jnp.bfloat16),
            pltpu.VMEM(weights.shape, jnp.bfloat16),
            pltpu.VMEM((2, weights.shape[2], width), jnp.bfloat16),
            pltpu.VMEM((2, 2 * pairs, width), jnp.bfloat16),
            pltpu.VMEM((2, lanes, width), jnp.bfloat16),
            pltpu.VMEM((tokens, 2 * pairs), jnp.float32),
            pltpu.VMEM((tp_count, tokens // tp_count, lanes), jnp.float32),
            pltpu.VMEM((tp_count, tokens // tp_count, lanes), jnp.float32),
            pltpu.VMEM((tp_count, tokens // tp_count, lanes), jnp.float32),
            pltpu.VMEM((tp_count, pairs, lanes), jnp.bfloat16),
            pltpu.VMEM((pairs, lanes), jnp.float32),
            pltpu.VMEM((sections, 8, EXAMPLES * number), jnp.float32),
            dma((2,)),
            dma((micro,)),
            dma((micro,)),
            dma((micro, ny)),
            dma((micro, ny)),
            dma((micro, max(ny - 1, 1))),
            dma((micro, max(ny - 1, 1))),
            dma((micro,)),
            dma((micro,)),
            dma((micro,)),
            dma((micro,)),
            dma((micro,)),
            dma,
            dma,
            dma,
            dma,
            dma,
            dma,
            dma,
            dma,
            dma,
        ],
        compiler_params=pltpu.CompilerParams(
            collective_id=0, has_side_effects=True, vmem_limit_bytes=56 * 2**20),
    )(
        top_cotangent, weights, layer_inputs, jnp.swapaxes(input_basis, 1, 2),
        jnp.swapaxes(output_basis, 1, 2), queries, sequence_example)


def solution(mesh):
    placed = (
        P("section", None, "tp"),
        P("section", "tp", None),
        P("section", "tp", None),
        P("section", "tp", None),
        P("section", "tp", None),
        P(),
        P(),
    )
    return jax.shard_map(
        shards, mesh=mesh, in_specs=placed, out_specs=P(None, "tp"), check_vma=False
    )
```

```python
import functools

import jax
import jax.numpy as jnp
from jax import lax
from jax.experimental import pallas as pl
from jax.experimental.pallas import tpu as pltpu
from jax.sharding import PartitionSpec as P

EXAMPLES = 2
ROWS = 32
TOP_ROUTED = (4, 11)
DIRECT = (11, 16)
LAGS = ((0, 0, 2, 3), (0, 1, 2, 3), (1, 2, 3, 4), (0, 1, 1, 1))
MESH = pl.DeviceIdType.MESH
NT = (((1,), (1,)), ((), ()))
NN = (((1,), (0,)), ((), ()))


def grid_of(tp_count):
    ny = 1
    while (2 * ny) * (2 * ny) <= tp_count:
        ny *= 2
    return tp_count // ny, ny


def slope_of(hidden):
    floats = hidden.astype(jnp.float32)
    logistic = jax.nn.sigmoid(floats)
    return logistic * (1.0 + floats * (1.0 - logistic))


def chain_kernel(
    sections, tp_count, top_ref, w_ref, h_ref, ib_ref, ob_ref, q_ref, se_ref, score_ref,
    buf_u, buf_m, buf_l, buf_v, w_v, w_t, ob_v, ib_v, out_v, part_in, got_in, full_in, grad_v, sum_v, score_v,
    w_sem, top_sem, recv_x, recv_u, recv_m, near_u, near_m, recv_v, send_u, send_m, send_l, send_v, send_my,
    part_send, part_recv, full_send, full_recv, grad_send, grad_recv, score_send, score_recv,
):
    nz, ny = grid_of(tp_count)
    sec = lax.axis_index("section")
    tp = lax.axis_index("tp")
    z, y = tp // ny, lax.rem(tp, ny)
    micro, _, rows, width = buf_u.shape
    is_top = sec == sections - 1
    has_lower = sec > 0
    pair_lower = lax.rem(sec, 2) == 1
    pair_upper = jnp.logical_not(pair_lower)
    helper = sections - 4

    def scaled(span):
        return [part * micro // 16 for part in span]

    def in_span(m, span):
        low, high = scaled(span)
        return jnp.logical_and(m >= low, m < high)

    def top_routed(m):
        return in_span(m, TOP_ROUTED if helper >= 0 else (0, 0))

    def direct(m):
        return in_span(m, DIRECT)

    far_fed = jnp.logical_and(pair_lower, jnp.logical_not(is_top))
    far_lower = jnp.logical_and(pair_upper, has_lower)

    far = [z]
    for k in range(nz - 1):
        down = nz - 1 - k
        from_low = down - (z >= down).astype(jnp.int32)
        from_high = k + (z <= k).astype(jnp.int32)
        far.append(jnp.where(z < nz // 2, from_low, from_high))
    near = far[:1] + far[:0:-1]
    mate = z + 1 - 2 * lax.rem(z, 2)

    def peer_z(step):
        return far[step] * ny + y

    def peer_y(step):
        return z * ny + lax.rem(y + step, ny)

    def src_at(zstep, ystep):
        return near[zstep] * ny + lax.rem(y + ystep, ny)

    def w_copy(layer):
        return pltpu.make_async_copy(w_ref.at[layer], w_v.at[layer], w_sem.at[layer])

    def top_copy(m, k):
        return pltpu.make_async_copy(
            top_ref.at[pl.ds(pl.multiple_of(m * rows, rows), rows), pl.ds(k * width, width)],
            buf_u.at[m, k], top_sem.at[m])

    def remote(src, dst, ssem, rsem, to_sec, to_tp):
        return pltpu.make_async_remote_copy(
            src_ref=src, dst_ref=dst, send_sem=ssem, recv_sem=rsem,
            device_id=(to_sec, to_tp), device_id_type=MESH)

    rank_in, rank_out = ib_ref.shape[1], ob_ref.shape[1]

    def prepare_bases():
        gap_in = jnp.zeros((rank_in, width), jnp.float32)
        gap_out = jnp.zeros((EXAMPLES * rank_out, width), jnp.float32)
        for layer in range(2):
            basis_in = ib_ref[layer].astype(jnp.float32)
            basis_out = [ob_ref[layer].astype(jnp.float32)] * EXAMPLES
            ins = [basis_in, gap_in] if layer == 0 else [gap_in, basis_in]
            outs = basis_out + [gap_out] if layer == 0 else [gap_out] + basis_out
            ib_v[layer] = jnp.concatenate(ins, 0).astype(jnp.bfloat16)
            ob_v[layer] = jnp.concatenate(outs, 0).astype(jnp.bfloat16)

    @pl.when(is_top)
    def _():
        @pl.loop(0, micro)
        def _(m):
            for k in range(tp_count):
                top_copy(m, k).start()

    w_copy(1).start()

    @pl.when(has_lower)
    def _():
        w_copy(0).start()

    barrier = pltpu.get_barrier_semaphore()

    def greet(to_sec, to_tp):
        pl.semaphore_signal(barrier, inc=1, device_id=(to_sec, to_tp), device_id_type=MESH)

    for step in range(1, tp_count):
        greet(sec, lax.rem(tp + step, tp_count))

    partner = sec + 1 - 2 * lax.rem(sec, 2)
    for step in range(1, nz):
        greet(partner, peer_z(step))
    for step in range(1, ny):
        greet(partner, peer_y(step))
    for step in range(1, sections):
        greet(lax.rem(sec + step, sections), tp)
    linked = 0
    for when, there in ((far_fed, sec + 1), (far_lower, sec - 1)):
        @pl.when(when)
        def _(there=there):
            for step in range(1, nz):
                greet(there, peer_z(step))
            for step in range(1, ny):
                greet(there, peer_y(step))

        linked = linked + (nz + ny - 2) * when.astype(jnp.int32)
    if helper >= 0:
        for here, there in ((sections - 1, helper), (helper, sections - 1)):
            @pl.when(sec == here)
            def _(there=there):
                for step in range(1, tp_count):
                    greet(there, lax.rem(tp + step, tp_count))

            linked = linked + (tp_count - 1) * (sec == here).astype(jnp.int32)

    def turn_weights(layer):
        w_copy(layer).wait()

        @pl.loop(0, tp_count)
        def _(k):
            columns = pl.ds(pl.multiple_of(k * width, width), width)
            w_t[layer, columns, :] = w_v[layer, :, columns].T

    prepare_bases()
    turn_weights(1)

    @pl.when(jnp.logical_and(has_lower, jnp.logical_not(is_top)))
    def _():
        turn_weights(0)

    pl.semaphore_wait(barrier, tp_count + nz + ny + sections - 4 + linked)

    def slots(buf, m, count, ssem, rsem):
        part = buf.at[m, pl.ds(0, count)]
        return remote(part, part, ssem, rsem, sec, tp)

    def relay_copy(buf, sends, recvs, m, zstep, ystep):
        src = src_at(zstep, 0)
        line = ny - ystep - (0 if zstep else 1)
        return remote(buf.at[m, src], buf.at[m, src], sends.at[m],
                      recvs.at[m, line], sec, peer_y(ystep))

    def forward_copy(buf, sends, recvs, m, ystep):
        src = src_at(0, ystep)
        return remote(buf.at[m, src], buf.at[m, src], sends.at[m],
                      recvs.at[m, ystep], sec, mate * ny + y)

    def spread_copy(buf, sends, recvs, m, zstep):
        return remote(buf.at[m, tp], buf.at[m, tp], sends.at[m], recvs.at[m, 0], sec, peer_z(zstep))

    def lower_own_copy(m):
        return remote(buf_l.at[m], buf_u.at[m, tp], send_l.at[m], recv_x.at[m], sec - 1, tp)

    def lower_z_copy(m, zstep):
        return remote(buf_l.at[m], buf_u.at[m, tp], send_l.at[m], recv_u.at[m, 0],
                      sec - 1, peer_z(zstep))

    def lower_y_copy(m, ystep):
        return remote(buf_l.at[m], buf_u.at[m, tp], send_l.at[m], near_u.at[m, ny - ystep - 1],
                      sec - 1, peer_y(ystep))

    def await_own(m):
        remote(buf_u.at[m, tp], buf_u.at[m, tp], send_my, recv_x.at[m], sec, tp).wait_recv()

    def await_line(buf, recvs, m, ystep):
        slots(buf, m, nz - 1, send_my, recvs.at[m, ystep]).wait_recv()

    def await_near(buf, nears, m, ystep):
        slots(buf, m, 1, send_my, nears.at[m, ystep - 1]).wait_recv()

    def pass_on(buf, sends, recvs, nears, m):
        for ystep in range(1, ny):
            await_near(buf, nears, m, ystep)
            forward_copy(buf, sends, recvs, m, ystep).start()
        await_line(buf, recvs, m, 0)
        for zstep in range(2, nz):
            for ystep in range(1, ny):
                relay_copy(buf, sends, recvs, m, zstep, ystep).start()

    def routed_on(buf, recvs, m, target):
        remote(buf_v.at[m], buf_v.at[m], send_my, recv_v.at[m], sec, tp).wait_recv()
        for zstep in range(nz - 1, 0, -1):
            remote(buf_v.at[m], buf.at[m, tp], send_v.at[m], recvs.at[m, 0],
                   target, src_at(zstep, 0)).start()

    def product(buf, m, layer, ystep, total=None):
        for zstep in range(nz):
            src = src_at(zstep, ystep)
            columns = pl.ds(pl.multiple_of(src * width, width), width)
            term = lax.dot_general(
                buf[m, src], w_t[layer, columns, :], NN, preferred_element_type=jnp.float32)
            total = term if total is None else total + term
        return total

    def upper(m):
        at = pl.ds(pl.multiple_of(m * rows, rows), rows)
        own = buf_u[m, tp]
        floats = own.astype(jnp.float32)
        slope = slope_of(h_ref[1, at, :])
        total = product(buf_u, m, 1, 0)
        for ystep in range(1, ny):
            @pl.when(jnp.logical_not(is_top))
            def _(ystep=ystep):
                await_line(buf_u, recv_u, m, ystep)

            total = product(buf_u, m, 1, ystep, total)
        middle = (floats + slope * total).astype(jnp.bfloat16)
        buf_m[m, tp] = middle

        routed = jnp.logical_and(is_top, top_routed(m))

        @pl.when(jnp.logical_and(has_lower, jnp.logical_not(routed)))
        def _():
            for step in range(1, nz):
                spread_copy(buf_m, send_m, recv_m, m, step).start()

        @pl.when(has_lower)
        def _():
            for step in range(1, ny):
                relay_copy(buf_m, send_m, near_m, m, 0, step).start()

        if helper >= 0:
            @pl.when(routed)
            def _():
                remote(buf_m.at[m, tp], buf_v.at[m], send_m.at[m], recv_v.at[m],
                       helper, tp).start()

        feats = lax.dot_general(
            own, ob_v[1], NT, preferred_element_type=jnp.float32
        ) + lax.dot_general(middle, ob_v[0], NT, preferred_element_type=jnp.float32)
        example = se_ref[m * rows // (micro * rows // se_ref.shape[0])]
        lane_example = lax.rem(
            lax.broadcasted_iota(jnp.int32, feats.shape, 1) // rank_out, EXAMPLES)
        out_v[at, :] = jnp.where(lane_example == example, feats, 0.0)

    def lower(m):
        at = pl.ds(pl.multiple_of(m * rows, rows), rows)
        floats = buf_m[m, tp].astype(jnp.float32)
        slope = slope_of(h_ref[0, at, :])

        total = product(buf_m, m, 0, 0)
        for ystep in range(1, ny):
            await_line(buf_m, recv_m, m, ystep)
            total = product(buf_m, m, 0, ystep, total)
        buf_l[m] = (floats + slope * total).astype(jnp.bfloat16)

        @pl.when(jnp.logical_or(pair_lower, direct(m)))
        def _():
            for step in range(1, nz):
                lower_z_copy(m, step).start()
            for step in range(1, ny):
                lower_y_copy(m, step).start()

        lower_own_copy(m).start()

    def tp_copy(src, dst, ssem, rsem, to_tp):
        return remote(src, dst, ssem, rsem, sec, to_tp)

    others = [(zstep, ystep) for zstep in [*range(nz - 1, 0, -1), 0]
              for ystep in range(ny) if zstep or ystep]

    def share(src_of, dst_ref, ssem, rsem):
        for zstep, ystep in others:
            to = src_at(zstep, ystep)
            tp_copy(src_of(to), dst_ref, ssem, rsem, to).start()

    def shared(buf, ssem, rsem):
        part = buf.at[pl.ds(0, tp_count - 1)]
        return tp_copy(part, part, ssem, rsem, tp)

    def score_copy(step):
        to = lax.rem(sec + step, sections)
        return remote(score_v.at[sec], score_v.at[sec], score_send,
                      score_recv, to, tp)

    def project_inputs():
        part_rows = part_in.shape[1]

        @pl.loop(0, tp_count)
        def _(k):
            at = pl.ds(pl.multiple_of(k * part_rows, part_rows), part_rows)
            total = None
            for layer in range(2):
                floats = h_ref[layer, at, :].astype(jnp.float32)
                activated = (floats * jax.nn.sigmoid(floats)).astype(jnp.bfloat16)
                term = lax.dot_general(
                    activated, ib_v[layer], NT, preferred_element_type=jnp.float32)
                total = term if total is None else total + term
            part_in[k] = total

        share(lambda to: part_in.at[to], got_in.at[tp], part_send, part_recv)
        total = part_in[tp]
        shared(got_in, send_my, part_recv).wait_recv()
        for step in range(1, tp_count):
            total = total + got_in[lax.rem(tp + step, tp_count)]
        full_in[tp] = total
        share(lambda to: full_in.at[tp], full_in.at[tp], full_send, full_recv)

    @pl.when(sec < sections // 2)
    def _():
        project_inputs()

    def spread_upper(m):
        await_own(m)
        for step in range(1, nz):
            spread_copy(buf_u, send_u, recv_u, m, step).start()
        for step in range(1, ny):
            relay_copy(buf_u, send_u, near_u, m, 0, step).start()

    def pass_upper(m):
        @pl.when(jnp.logical_or(pair_upper, direct(m)))
        def _():
            await_own(m)

        pass_on(buf_u, send_u, recv_u, near_u, m)

    def pass_middle(m):
        pass_on(buf_m, send_m, recv_m, near_m, m)

    def within(m):
        return jnp.logical_and(m >= 0, m < micro)

    kind = jnp.where(is_top, 0, jnp.where(far_fed, 2, jnp.where(has_lower, 1, 3)))

    def lag_of(k):
        lag = LAGS[0][k]
        for other in range(1, 4):
            lag = jnp.where(kind == other, LAGS[other][k], lag)
        return lag

    lag_pass, lag_upper, lag_middle, lag_lower = [lag_of(k) for k in range(4)]
    steps = micro + max(max(lags) for lags in LAGS)

    if helper >= 0:
        @pl.when(sec == helper)
        def _():
            @pl.loop(*scaled(TOP_ROUTED))
            def _(m):
                routed_on(buf_m, recv_m, m, sections - 1)

    @pl.loop(0, steps)
    def _(it):
        m_pass = it - lag_pass
        m_up = it - lag_upper
        m_mid = it - lag_middle
        m_low = it - lag_lower

        @pl.when(jnp.logical_and(jnp.logical_and(it < micro, far_fed), jnp.logical_not(direct(it))))
        def _():
            spread_upper(it)

        @pl.when(jnp.logical_and(within(m_pass), jnp.logical_not(is_top)))
        def _():
            pass_upper(m_pass)

        @pl.when(within(m_up))
        def _():
            @pl.when(is_top)
            def _():
                pltpu.make_async_copy(
                    buf_u.at[m_up], buf_u.at[m_up], top_sem.at[m_up]).wait()

            upper(m_up)

        @pl.when(jnp.logical_and(it == 0, is_top))
        def _():
            turn_weights(0)

        @pl.when(jnp.logical_and(within(m_mid), has_lower))
        def _():
            pass_middle(m_mid)

        @pl.when(jnp.logical_and(within(m_low), has_lower))
        def _():
            lower(m_low)

    @pl.when(sec >= sections // 2)
    def _():
        project_inputs()

    shared(full_in, send_my, full_recv).wait_recv()
    lanes = 2 * rank_in
    pairs = EXAMPLES * rank_out
    product_all = lax.dot_general(
        out_v[...], full_in[...].reshape(micro * rows, lanes), (((0,), (0,)), ((), ())),
        precision=lax.Precision.HIGHEST, preferred_element_type=jnp.float32)
    lane = lax.broadcasted_iota(jnp.int32, (pairs, lanes), 1)
    own_grad = jnp.where(lane < rank_in, product_all[:pairs], product_all[pairs:])
    grad_v[tp] = own_grad.astype(jnp.bfloat16)
    share(lambda to: grad_v.at[tp], grad_v.at[tp], grad_send, grad_recv)
    shared(grad_v, send_my, grad_recv).wait_recv()
    total = grad_v[0].astype(jnp.float32)
    for k in range(1, tp_count):
        total = total + grad_v[k].astype(jnp.float32)
    sum_v[...] = total
    half = rank_out // 2
    number = q_ref.shape[1]
    sums = []
    for example in range(EXAMPLES):
        even = sum_v[pl.ds(example * rank_out, half, stride=2), :]
        odd = sum_v[pl.ds(example * rank_out + 1, half, stride=2), :]
        acc = jnp.zeros((number, lanes), jnp.float32)
        for layer in range(2):
            part = slice(layer * rank_in, (layer + 1) * rank_in)
            tiles = jnp.concatenate([even[:, part], odd[:, part]], 1)
            for j in range(half):
                block = q_ref[layer, :, j * lanes:(j + 1) * lanes].astype(jnp.float32)
                acc = acc + tiles[j:j + 1, :] * block
        sums.append(acc)
    score_v[sec] = lax.dot_general(
        jnp.ones((8, lanes), jnp.float32), jnp.concatenate(sums, 0), NT,
        precision=lax.Precision.HIGHEST, preferred_element_type=jnp.float32)
    for step in range(1, sections):
        score_copy(step).start()
    scores = score_v.at[pl.ds(0, sections - 1)]
    remote(scores, scores, send_my, score_recv, sec, tp).wait_recv()
    total = score_v[0]
    for k in range(1, sections):
        total = total + score_v[k]
    for example in range(EXAMPLES):
        score_ref[example:example + 1, :] = total[0:1, example * number:(example + 1) * number]

    shared(part_in, part_send, send_my).wait_send()
    shared(full_in, full_send, send_my).wait_send()
    shared(grad_v, grad_send, send_my).wait_send()
    remote(scores, scores, score_send, send_my, sec, tp).wait_send()

    def sent(sends, buf, m, count, when):
        @pl.when(when)
        def _():
            slots(buf, m, count, sends.at[m], send_my).wait_send()

    @pl.loop(0, micro)
    def _(m):
        top_far = jnp.logical_and(is_top, top_routed(m))
        spread = jnp.logical_and(far_fed, jnp.logical_not(direct(m)))
        hop = jnp.logical_and(far_lower, jnp.logical_not(direct(m)))
        sent(send_u, buf_u, m, tp_count - 1, spread)
        if ny > 1:
            sent(send_u, buf_u, m, (nz - 1) * (ny - 1),
                 jnp.logical_not(jnp.logical_or(is_top, spread)))
        sent(send_m, buf_m, m, tp_count - 1, jnp.logical_and(has_lower, jnp.logical_not(top_far)))
        sent(send_m, buf_m, m, 1 + nz * (ny - 1), top_far)
        sent(send_l, buf_u, m, nz + ny - 1, jnp.logical_and(has_lower, jnp.logical_not(hop)))
        sent(send_l, buf_u, m, 1, hop)
        if helper >= 0:
            sent(send_v, buf_u, m, nz - 1,
                 jnp.logical_and(sec == helper, top_routed(m)))


def shards(
    layer_inputs, weights, input_basis, output_basis, queries, top_cotangent, sequence_example
):
    sections = lax.axis_size("section")
    tp_count = lax.axis_size("tp")
    tokens, width = layer_inputs.shape[1:]
    rows = ROWS
    micro = tokens // rows
    nz, ny = grid_of(tp_count)
    lanes = 2 * input_basis.shape[2]
    pairs = EXAMPLES * output_basis.shape[2]
    number = queries.shape[1]
    dma = pltpu.SemaphoreType.DMA
    vmem = pl.BlockSpec(memory_space=pltpu.VMEM)
    hbm = pl.BlockSpec(memory_space=pl.ANY)
    smem = pl.BlockSpec(memory_space=pltpu.SMEM)
    return pl.pallas_call(
        functools.partial(chain_kernel, sections, tp_count),
        out_shape=jax.ShapeDtypeStruct((EXAMPLES, number), jnp.float32),
        in_specs=[hbm, hbm, vmem, vmem, vmem, vmem, smem],
        out_specs=vmem,
        scratch_shapes=[
            pltpu.VMEM((micro, tp_count, rows, width), jnp.bfloat16),
            pltpu.VMEM((micro, tp_count, rows, width), jnp.bfloat16),
            pltpu.VMEM((micro, rows, width), jnp.bfloat16),
            pltpu.VMEM((micro, rows, width), jnp.bfloat16),
            pltpu.VMEM(weights.shape, jnp.bfloat16),
            pltpu.VMEM((2, weights.shape[2], width), jnp.bfloat16),
            pltpu.VMEM((2, 2 * pairs, width), jnp.bfloat16),
            pltpu.VMEM((2, lanes, width), jnp.bfloat16),
            pltpu.VMEM((tokens, 2 * pairs), jnp.float32),
            pltpu.VMEM((tp_count, tokens // tp_count, lanes), jnp.float32),
            pltpu.VMEM((tp_count, tokens // tp_count, lanes), jnp.float32),
            pltpu.VMEM((tp_count, tokens // tp_count, lanes), jnp.float32),
            pltpu.VMEM((tp_count, pairs, lanes), jnp.bfloat16),
            pltpu.VMEM((pairs, lanes), jnp.float32),
            pltpu.VMEM((sections, 8, EXAMPLES * number), jnp.float32),
            dma((2,)),
            dma((micro,)),
            dma((micro,)),
            dma((micro, ny)),
            dma((micro, ny)),
            dma((micro, max(ny - 1, 1))),
            dma((micro, max(ny - 1, 1))),
            dma((micro,)),
            dma((micro,)),
            dma((micro,)),
            dma((micro,)),
            dma((micro,)),
            dma,
            dma,
            dma,
            dma,
            dma,
            dma,
            dma,
            dma,
            dma,
        ],
        compiler_params=pltpu.CompilerParams(
            collective_id=0, has_side_effects=True, vmem_limit_bytes=56 * 2**20),
    )(
        top_cotangent, weights, layer_inputs, jnp.swapaxes(input_basis, 1, 2),
        jnp.swapaxes(output_basis, 1, 2), queries, sequence_example)


def solution(mesh):
    placed = (
        P("section", None, "tp"),
        P("section", "tp", None),
        P("section", "tp", None),
        P("section", "tp", None),
        P("section", "tp", None),
        P(),
        P(),
    )
    return jax.shard_map(
        shards, mesh=mesh, in_specs=placed, out_specs=P(None, "tp"), check_vma=False
    )
```

```python
import functools

import jax
import jax.numpy as jnp
from jax import lax
from jax.experimental import pallas as pl
from jax.experimental.pallas import tpu as pltpu
from jax.sharding import PartitionSpec as P

EXAMPLES = 2
ROWS = 32
TOP_ROUTED = (4, 12)
DIRECT = (11, 16)
LAGS = ((0, 0, 2, 3), (0, 1, 2, 3), (1, 2, 3, 4), (0, 1, 1, 1))
MESH = pl.DeviceIdType.MESH
NT = (((1,), (1,)), ((), ()))
NN = (((1,), (0,)), ((), ()))


def grid_of(tp_count):
    ny = 1
    while (2 * ny) * (2 * ny) <= tp_count:
        ny *= 2
    return tp_count // ny, ny


def slope_of(hidden):
    floats = hidden.astype(jnp.float32)
    logistic = jax.nn.sigmoid(floats)
    return logistic * (1.0 + floats * (1.0 - logistic))


def chain_kernel(
    sections, tp_count, top_ref, w_ref, h_ref, ib_ref, ob_ref, q_ref, se_ref, score_ref,
    buf_u, buf_m, buf_l, buf_v, w_v, w_t, ob_v, ib_v, out_v, part_in, got_in, full_in, grad_v, sum_v, score_v,
    w_sem, top_sem, recv_x, recv_u, recv_m, near_u, near_m, recv_v, send_u, send_m, send_l, send_v, send_my,
    part_send, part_recv, full_send, full_recv, grad_send, grad_recv, score_send, score_recv,
):
    nz, ny = grid_of(tp_count)
    sec = lax.axis_index("section")
    tp = lax.axis_index("tp")
    z, y = tp // ny, lax.rem(tp, ny)
    micro, _, rows, width = buf_u.shape
    is_top = sec == sections - 1
    has_lower = sec > 0
    pair_lower = lax.rem(sec, 2) == 1
    pair_upper = jnp.logical_not(pair_lower)
    helper = sections - 4

    def scaled(span):
        return [part * micro // 16 for part in span]

    def in_span(m, span):
        low, high = scaled(span)
        return jnp.logical_and(m >= low, m < high)

    def top_routed(m):
        return in_span(m, TOP_ROUTED if helper >= 0 else (0, 0))

    def direct(m):
        return in_span(m, DIRECT)

    far_fed = jnp.logical_and(pair_lower, jnp.logical_not(is_top))
    far_lower = jnp.logical_and(pair_upper, has_lower)

    far = [z]
    for k in range(nz - 1):
        down = nz - 1 - k
        from_low = down - (z >= down).astype(jnp.int32)
        from_high = k + (z <= k).astype(jnp.int32)
        far.append(jnp.where(z < nz // 2, from_low, from_high))
    near = far[:1] + far[:0:-1]
    mate = z + 1 - 2 * lax.rem(z, 2)

    def peer_z(step):
        return far[step] * ny + y

    def peer_y(step):
        return z * ny + lax.rem(y + step, ny)

    def src_at(zstep, ystep):
        return near[zstep] * ny + lax.rem(y + ystep, ny)

    def w_copy(layer):
        return pltpu.make_async_copy(w_ref.at[layer], w_v.at[layer], w_sem.at[layer])

    def top_copy(m, k):
        return pltpu.make_async_copy(
            top_ref.at[pl.ds(pl.multiple_of(m * rows, rows), rows), pl.ds(k * width, width)],
            buf_u.at[m, k], top_sem.at[m])

    def remote(src, dst, ssem, rsem, to_sec, to_tp):
        return pltpu.make_async_remote_copy(
            src_ref=src, dst_ref=dst, send_sem=ssem, recv_sem=rsem,
            device_id=(to_sec, to_tp), device_id_type=MESH)

    rank_in, rank_out = ib_ref.shape[1], ob_ref.shape[1]

    def prepare_bases():
        gap_in = jnp.zeros((rank_in, width), jnp.float32)
        gap_out = jnp.zeros((EXAMPLES * rank_out, width), jnp.float32)
        for layer in range(2):
            basis_in = ib_ref[layer].astype(jnp.float32)
            basis_out = [ob_ref[layer].astype(jnp.float32)] * EXAMPLES
            ins = [basis_in, gap_in] if layer == 0 else [gap_in, basis_in]
            outs = basis_out + [gap_out] if layer == 0 else [gap_out] + basis_out
            ib_v[layer] = jnp.concatenate(ins, 0).astype(jnp.bfloat16)
            ob_v[layer] = jnp.concatenate(outs, 0).astype(jnp.bfloat16)

    @pl.when(is_top)
    def _():
        @pl.loop(0, micro)
        def _(m):
            for k in range(tp_count):
                top_copy(m, k).start()

    w_copy(1).start()

    @pl.when(has_lower)
    def _():
        w_copy(0).start()

    barrier = pltpu.get_barrier_semaphore()

    def greet(to_sec, to_tp):
        pl.semaphore_signal(barrier, inc=1, device_id=(to_sec, to_tp), device_id_type=MESH)

    for step in range(1, tp_count):
        greet(sec, lax.rem(tp + step, tp_count))

    partner = sec + 1 - 2 * lax.rem(sec, 2)
    for step in range(1, nz):
        greet(partner, peer_z(step))
    for step in range(1, ny):
        greet(partner, peer_y(step))
    for step in range(1, sections):
        greet(lax.rem(sec + step, sections), tp)
    linked = 0
    for when, there in ((far_fed, sec + 1), (far_lower, sec - 1)):
        @pl.when(when)
        def _(there=there):
            for step in range(1, nz):
                greet(there, peer_z(step))
            for step in range(1, ny):
                greet(there, peer_y(step))

        linked = linked + (nz + ny - 2) * when.astype(jnp.int32)
    if helper >= 0:
        for here, there in ((sections - 1, helper), (helper, sections - 1)):
            @pl.when(sec == here)
            def _(there=there):
                for step in range(1, tp_count):
                    greet(there, lax.rem(tp + step, tp_count))

            linked = linked + (tp_count - 1) * (sec == here).astype(jnp.int32)

    def turn_weights(layer):
        w_copy(layer).wait()

        @pl.loop(0, tp_count)
        def _(k):
            columns = pl.ds(pl.multiple_of(k * width, width), width)
            w_t[layer, columns, :] = w_v[layer, :, columns].T

    prepare_bases()
    turn_weights(1)

    @pl.when(jnp.logical_and(has_lower, jnp.logical_not(is_top)))
    def _():
        turn_weights(0)

    pl.semaphore_wait(barrier, tp_count + nz + ny + sections - 4 + linked)

    def slots(buf, m, count, ssem, rsem):
        part = buf.at[m, pl.ds(0, count)]
        return remote(part, part, ssem, rsem, sec, tp)

    def relay_copy(buf, sends, recvs, m, zstep, ystep):
        src = src_at(zstep, 0)
        line = ny - ystep - (0 if zstep else 1)
        return remote(buf.at[m, src], buf.at[m, src], sends.at[m],
                      recvs.at[m, line], sec, peer_y(ystep))

    def forward_copy(buf, sends, recvs, m, ystep):
        src = src_at(0, ystep)
        return remote(buf.at[m, src], buf.at[m, src], sends.at[m],
                      recvs.at[m, ystep], sec, mate * ny + y)

    def spread_copy(buf, sends, recvs, m, zstep):
        return remote(buf.at[m, tp], buf.at[m, tp], sends.at[m], recvs.at[m, 0], sec, peer_z(zstep))

    def lower_own_copy(m):
        return remote(buf_l.at[m], buf_u.at[m, tp], send_l.at[m], recv_x.at[m], sec - 1, tp)

    def lower_z_copy(m, zstep):
        return remote(buf_l.at[m], buf_u.at[m, tp], send_l.at[m], recv_u.at[m, 0],
                      sec - 1, peer_z(zstep))

    def lower_y_copy(m, ystep):
        return remote(buf_l.at[m], buf_u.at[m, tp], send_l.at[m], near_u.at[m, ny - ystep - 1],
                      sec - 1, peer_y(ystep))

    def await_own(m):
        remote(buf_u.at[m, tp], buf_u.at[m, tp], send_my, recv_x.at[m], sec, tp).wait_recv()

    def await_line(buf, recvs, m, ystep):
        slots(buf, m, nz - 1, send_my, recvs.at[m, ystep]).wait_recv()

    def await_near(buf, nears, m, ystep):
        slots(buf, m, 1, send_my, nears.at[m, ystep - 1]).wait_recv()

    def pass_on(buf, sends, recvs, nears, m):
        for ystep in range(1, ny):
            await_near(buf, nears, m, ystep)
            forward_copy(buf, sends, recvs, m, ystep).start()
        await_line(buf, recvs, m, 0)
        for zstep in range(2, nz):
            for ystep in range(1, ny):
                relay_copy(buf, sends, recvs, m, zstep, ystep).start()

    def routed_on(buf, recvs, m, target):
        remote(buf_v.at[m], buf_v.at[m], send_my, recv_v.at[m], sec, tp).wait_recv()
        for zstep in range(nz - 1, 0, -1):
            remote(buf_v.at[m], buf.at[m, tp], send_v.at[m], recvs.at[m, 0],
                   target, src_at(zstep, 0)).start()

    def product(buf, m, layer, ystep, total=None):
        for zstep in range(nz):
            src = src_at(zstep, ystep)
            columns = pl.ds(pl.multiple_of(src * width, width), width)
            term = lax.dot_general(
                buf[m, src], w_t[layer, columns, :], NN, preferred_element_type=jnp.float32)
            total = term if total is None else total + term
        return total

    def upper(m):
        at = pl.ds(pl.multiple_of(m * rows, rows), rows)
        own = buf_u[m, tp]
        floats = own.astype(jnp.float32)
        slope = slope_of(h_ref[1, at, :])
        total = product(buf_u, m, 1, 0)
        for ystep in range(1, ny):
            @pl.when(jnp.logical_not(is_top))
            def _(ystep=ystep):
                await_line(buf_u, recv_u, m, ystep)

            total = product(buf_u, m, 1, ystep, total)
        middle = (floats + slope * total).astype(jnp.bfloat16)
        buf_m[m, tp] = middle

        routed = jnp.logical_and(is_top, top_routed(m))

        @pl.when(jnp.logical_and(has_lower, jnp.logical_not(routed)))
        def _():
            for step in range(1, nz):
                spread_copy(buf_m, send_m, recv_m, m, step).start()

        @pl.when(has_lower)
        def _():
            for step in range(1, ny):
                relay_copy(buf_m, send_m, near_m, m, 0, step).start()

        if helper >= 0:
            @pl.when(routed)
            def _():
                remote(buf_m.at[m, tp], buf_v.at[m], send_m.at[m], recv_v.at[m],
                       helper, tp).start()

        feats = lax.dot_general(
            own, ob_v[1], NT, preferred_element_type=jnp.float32
        ) + lax.dot_general(middle, ob_v[0], NT, preferred_element_type=jnp.float32)
        example = se_ref[m * rows // (micro * rows // se_ref.shape[0])]
        lane_example = lax.rem(
            lax.broadcasted_iota(jnp.int32, feats.shape, 1) // rank_out, EXAMPLES)
        out_v[at, :] = jnp.where(lane_example == example, feats, 0.0)

    def lower(m):
        at = pl.ds(pl.multiple_of(m * rows, rows), rows)
        floats = buf_m[m, tp].astype(jnp.float32)
        slope = slope_of(h_ref[0, at, :])

        total = product(buf_m, m, 0, 0)
        for ystep in range(1, ny):
            await_line(buf_m, recv_m, m, ystep)
            total = product(buf_m, m, 0, ystep, total)
        buf_l[m] = (floats + slope * total).astype(jnp.bfloat16)

        @pl.when(jnp.logical_or(pair_lower, direct(m)))
        def _():
            for step in range(1, nz):
                lower_z_copy(m, step).start()
            for step in range(1, ny):
                lower_y_copy(m, step).start()

        lower_own_copy(m).start()

    def tp_copy(src, dst, ssem, rsem, to_tp):
        return remote(src, dst, ssem, rsem, sec, to_tp)

    others = [(zstep, ystep) for zstep in [*range(nz - 1, 0, -1), 0]
              for ystep in range(ny) if zstep or ystep]

    def share(src_of, dst_ref, ssem, rsem):
        for zstep, ystep in others:
            to = src_at(zstep, ystep)
            tp_copy(src_of(to), dst_ref, ssem, rsem, to).start()

    def shared(buf, ssem, rsem):
        part = buf.at[pl.ds(0, tp_count - 1)]
        return tp_copy(part, part, ssem, rsem, tp)

    def score_copy(step):
        to = lax.rem(sec + step, sections)
        return remote(score_v.at[sec], score_v.at[sec], score_send,
                      score_recv, to, tp)

    def project_inputs():
        part_rows = part_in.shape[1]

        @pl.loop(0, tp_count)
        def _(k):
            at = pl.ds(pl.multiple_of(k * part_rows, part_rows), part_rows)
            total = None
            for layer in range(2):
                floats = h_ref[layer, at, :].astype(jnp.float32)
                activated = (floats * jax.nn.sigmoid(floats)).astype(jnp.bfloat16)
                term = lax.dot_general(
                    activated, ib_v[layer], NT, preferred_element_type=jnp.float32)
                total = term if total is None else total + term
            part_in[k] = total

        share(lambda to: part_in.at[to], got_in.at[tp], part_send, part_recv)
        total = part_in[tp]
        shared(got_in, send_my, part_recv).wait_recv()
        for step in range(1, tp_count):
            total = total + got_in[lax.rem(tp + step, tp_count)]
        full_in[tp] = total
        share(lambda to: full_in.at[tp], full_in.at[tp], full_send, full_recv)

    @pl.when(sec < sections // 2)
    def _():
        project_inputs()

    def spread_upper(m):
        await_own(m)
        for step in range(1, nz):
            spread_copy(buf_u, send_u, recv_u, m, step).start()
        for step in range(1, ny):
            relay_copy(buf_u, send_u, near_u, m, 0, step).start()

    def pass_upper(m):
        @pl.when(jnp.logical_or(pair_upper, direct(m)))
        def _():
            await_own(m)

        pass_on(buf_u, send_u, recv_u, near_u, m)

    def pass_middle(m):
        pass_on(buf_m, send_m, recv_m, near_m, m)

    def within(m):
        return jnp.logical_and(m >= 0, m < micro)

    kind = jnp.where(is_top, 0, jnp.where(far_fed, 2, jnp.where(has_lower, 1, 3)))

    def lag_of(k):
        lag = LAGS[0][k]
        for other in range(1, 4):
            lag = jnp.where(kind == other, LAGS[other][k], lag)
        return lag

    lag_pass, lag_upper, lag_middle, lag_lower = [lag_of(k) for k in range(4)]
    steps = micro + max(max(lags) for lags in LAGS)

    if helper >= 0:
        @pl.when(sec == helper)
        def _():
            @pl.loop(*scaled(TOP_ROUTED))
            def _(m):
                routed_on(buf_m, recv_m, m, sections - 1)

    @pl.loop(0, steps)
    def _(it):
        m_pass = it - lag_pass
        m_up = it - lag_upper
        m_mid = it - lag_middle
        m_low = it - lag_lower

        @pl.when(jnp.logical_and(jnp.logical_and(it < micro, far_fed), jnp.logical_not(direct(it))))
        def _():
            spread_upper(it)

        @pl.when(jnp.logical_and(within(m_pass), jnp.logical_not(is_top)))
        def _():
            pass_upper(m_pass)

        @pl.when(within(m_up))
        def _():
            @pl.when(is_top)
            def _():
                pltpu.make_async_copy(
                    buf_u.at[m_up], buf_u.at[m_up], top_sem.at[m_up]).wait()

            upper(m_up)

        @pl.when(jnp.logical_and(it == 0, is_top))
        def _():
            turn_weights(0)

        @pl.when(jnp.logical_and(within(m_mid), has_lower))
        def _():
            pass_middle(m_mid)

        @pl.when(jnp.logical_and(within(m_low), has_lower))
        def _():
            lower(m_low)

    @pl.when(sec >= sections // 2)
    def _():
        project_inputs()

    shared(full_in, send_my, full_recv).wait_recv()
    lanes = 2 * rank_in
    pairs = EXAMPLES * rank_out
    product_all = lax.dot_general(
        out_v[...], full_in[...].reshape(micro * rows, lanes), (((0,), (0,)), ((), ())),
        precision=lax.Precision.HIGHEST, preferred_element_type=jnp.float32)
    lane = lax.broadcasted_iota(jnp.int32, (pairs, lanes), 1)
    own_grad = jnp.where(lane < rank_in, product_all[:pairs], product_all[pairs:])
    grad_v[tp] = own_grad.astype(jnp.bfloat16)
    share(lambda to: grad_v.at[tp], grad_v.at[tp], grad_send, grad_recv)
    shared(grad_v, send_my, grad_recv).wait_recv()
    total = grad_v[0].astype(jnp.float32)
    for k in range(1, tp_count):
        total = total + grad_v[k].astype(jnp.float32)
    sum_v[...] = total
    half = rank_out // 2
    number = q_ref.shape[1]
    sums = []
    for example in range(EXAMPLES):
        even = sum_v[pl.ds(example * rank_out, half, stride=2), :]
        odd = sum_v[pl.ds(example * rank_out + 1, half, stride=2), :]
        acc = jnp.zeros((number, lanes), jnp.float32)
        for layer in range(2):
            part = slice(layer * rank_in, (layer + 1) * rank_in)
            tiles = jnp.concatenate([even[:, part], odd[:, part]], 1)
            for j in range(half):
                block = q_ref[layer, :, j * lanes:(j + 1) * lanes].astype(jnp.float32)
                acc = acc + tiles[j:j + 1, :] * block
        sums.append(acc)
    score_v[sec] = lax.dot_general(
        jnp.ones((8, lanes), jnp.float32), jnp.concatenate(sums, 0), NT,
        precision=lax.Precision.HIGHEST, preferred_element_type=jnp.float32)
    for step in range(1, sections):
        score_copy(step).start()
    shared(part_in, part_send, send_my).wait_send()
    shared(full_in, full_send, send_my).wait_send()
    shared(grad_v, grad_send, send_my).wait_send()

    def sent(sends, buf, m, count, when):
        @pl.when(when)
        def _():
            slots(buf, m, count, sends.at[m], send_my).wait_send()

    @pl.loop(0, micro)
    def _(m):
        top_far = jnp.logical_and(is_top, top_routed(m))
        spread = jnp.logical_and(far_fed, jnp.logical_not(direct(m)))
        hop = jnp.logical_and(far_lower, jnp.logical_not(direct(m)))
        sent(send_u, buf_u, m, tp_count - 1, spread)
        if ny > 1:
            sent(send_u, buf_u, m, (nz - 1) * (ny - 1),
                 jnp.logical_not(jnp.logical_or(is_top, spread)))
        sent(send_m, buf_m, m, tp_count - 1, jnp.logical_and(has_lower, jnp.logical_not(top_far)))
        sent(send_m, buf_m, m, 1 + nz * (ny - 1), top_far)
        sent(send_l, buf_u, m, nz + ny - 1, jnp.logical_and(has_lower, jnp.logical_not(hop)))
        sent(send_l, buf_u, m, 1, hop)
        if helper >= 0:
            sent(send_v, buf_u, m, nz - 1,
                 jnp.logical_and(sec == helper, top_routed(m)))

    scores = score_v.at[pl.ds(0, sections - 1)]
    remote(scores, scores, send_my, score_recv, sec, tp).wait_recv()
    total = score_v[0]
    for k in range(1, sections):
        total = total + score_v[k]
    for example in range(EXAMPLES):
        score_ref[example:example + 1, :] = total[0:1, example * number:(example + 1) * number]
    remote(scores, scores, score_send, send_my, sec, tp).wait_send()


def shards(
    layer_inputs, weights, input_basis, output_basis, queries, top_cotangent, sequence_example
):
    sections = lax.axis_size("section")
    tp_count = lax.axis_size("tp")
    tokens, width = layer_inputs.shape[1:]
    rows = ROWS
    micro = tokens // rows
    nz, ny = grid_of(tp_count)
    lanes = 2 * input_basis.shape[2]
    pairs = EXAMPLES * output_basis.shape[2]
    number = queries.shape[1]
    dma = pltpu.SemaphoreType.DMA
    vmem = pl.BlockSpec(memory_space=pltpu.VMEM)
    hbm = pl.BlockSpec(memory_space=pl.ANY)
    smem = pl.BlockSpec(memory_space=pltpu.SMEM)
    return pl.pallas_call(
        functools.partial(chain_kernel, sections, tp_count),
        out_shape=jax.ShapeDtypeStruct((EXAMPLES, number), jnp.float32),
        in_specs=[hbm, hbm, vmem, vmem, vmem, vmem, smem],
        out_specs=vmem,
        scratch_shapes=[
            pltpu.VMEM((micro, tp_count, rows, width), jnp.bfloat16),
            pltpu.VMEM((micro, tp_count, rows, width), jnp.bfloat16),
            pltpu.VMEM((micro, rows, width), jnp.bfloat16),
            pltpu.VMEM((micro, rows, width), jnp.bfloat16),
            pltpu.VMEM(weights.shape, jnp.bfloat16),
            pltpu.VMEM((2, weights.shape[2], width), jnp.bfloat16),
            pltpu.VMEM((2, 2 * pairs, width), jnp.bfloat16),
            pltpu.VMEM((2, lanes, width), jnp.bfloat16),
            pltpu.VMEM((tokens, 2 * pairs), jnp.float32),
            pltpu.VMEM((tp_count, tokens // tp_count, lanes), jnp.float32),
            pltpu.VMEM((tp_count, tokens // tp_count, lanes), jnp.float32),
            pltpu.VMEM((tp_count, tokens // tp_count, lanes), jnp.float32),
            pltpu.VMEM((tp_count, pairs, lanes), jnp.bfloat16),
            pltpu.VMEM((pairs, lanes), jnp.float32),
            pltpu.VMEM((sections, 8, EXAMPLES * number), jnp.float32),
            dma((2,)),
            dma((micro,)),
            dma((micro,)),
            dma((micro, ny)),
            dma((micro, ny)),
            dma((micro, max(ny - 1, 1))),
            dma((micro, max(ny - 1, 1))),
            dma((micro,)),
            dma((micro,)),
            dma((micro,)),
            dma((micro,)),
            dma((micro,)),
            dma,
            dma,
            dma,
            dma,
            dma,
            dma,
            dma,
            dma,
            dma,
        ],
        compiler_params=pltpu.CompilerParams(
            collective_id=0, has_side_effects=True, vmem_limit_bytes=56 * 2**20),
    )(
        top_cotangent, weights, layer_inputs, jnp.swapaxes(input_basis, 1, 2),
        jnp.swapaxes(output_basis, 1, 2), queries, sequence_example)


def solution(mesh):
    placed = (
        P("section", None, "tp"),
        P("section", "tp", None),
        P("section", "tp", None),
        P("section", "tp", None),
        P("section", "tp", None),
        P(),
        P(),
    )
    return jax.shard_map(
        shards, mesh=mesh, in_specs=placed, out_specs=P(None, "tp"), check_vma=False
    )
```

```python
import functools

import jax
import jax.numpy as jnp
from jax import lax
from jax.experimental import pallas as pl
from jax.experimental.pallas import tpu as pltpu
from jax.sharding import PartitionSpec as P

EXAMPLES = 2
ROWS = 32
TOP_ROUTED = (5, 13)
DIRECT = (11, 16)
LAGS = ((0, 0, 2, 3), (0, 1, 2, 3), (1, 2, 3, 4), (0, 1, 1, 1))
MESH = pl.DeviceIdType.MESH
NT = (((1,), (1,)), ((), ()))
NN = (((1,), (0,)), ((), ()))


def grid_of(tp_count):
    ny = 1
    while (2 * ny) * (2 * ny) <= tp_count:
        ny *= 2
    return tp_count // ny, ny


def slope_of(hidden):
    floats = hidden.astype(jnp.float32)
    logistic = jax.nn.sigmoid(floats)
    return logistic * (1.0 + floats * (1.0 - logistic))


def chain_kernel(
    sections, tp_count, top_ref, w_ref, h_ref, ib_ref, ob_ref, q_ref, se_ref, score_ref,
    buf_u, buf_m, buf_l, buf_v, w_v, w_t, ob_v, ib_v, out_v, part_in, got_in, full_in, grad_v, sum_v, score_v,
    w_sem, top_sem, recv_x, recv_u, recv_m, near_u, near_m, recv_v, send_u, send_m, send_l, send_v, send_my,
    part_send, part_recv, full_send, full_recv, grad_send, grad_recv, score_send, score_recv,
):
    nz, ny = grid_of(tp_count)
    sec = lax.axis_index("section")
    tp = lax.axis_index("tp")
    z, y = tp // ny, lax.rem(tp, ny)
    micro, _, rows, width = buf_u.shape
    is_top = sec == sections - 1
    has_lower = sec > 0
    pair_lower = lax.rem(sec, 2) == 1
    pair_upper = jnp.logical_not(pair_lower)
    helper = sections - 4

    def scaled(span):
        return [part * micro // 16 for part in span]

    def in_span(m, span):
        low, high = scaled(span)
        return jnp.logical_and(m >= low, m < high)

    def top_routed(m):
        return in_span(m, TOP_ROUTED if helper >= 0 else (0, 0))

    def direct(m):
        return in_span(m, DIRECT)

    far_fed = jnp.logical_and(pair_lower, jnp.logical_not(is_top))
    far_lower = jnp.logical_and(pair_upper, has_lower)

    far = [z]
    for k in range(nz - 1):
        down = nz - 1 - k
        from_low = down - (z >= down).astype(jnp.int32)
        from_high = k + (z <= k).astype(jnp.int32)
        far.append(jnp.where(z < nz // 2, from_low, from_high))
    near = far[:1] + far[:0:-1]
    mate = z + 1 - 2 * lax.rem(z, 2)

    def peer_z(step):
        return far[step] * ny + y

    def peer_y(step):
        return z * ny + lax.rem(y + step, ny)

    def src_at(zstep, ystep):
        return near[zstep] * ny + lax.rem(y + ystep, ny)

    def w_copy(layer):
        return pltpu.make_async_copy(w_ref.at[layer], w_v.at[layer], w_sem.at[layer])

    def top_copy(m, k):
        return pltpu.make_async_copy(
            top_ref.at[pl.ds(pl.multiple_of(m * rows, rows), rows), pl.ds(k * width, width)],
            buf_u.at[m, k], top_sem.at[m])

    def remote(src, dst, ssem, rsem, to_sec, to_tp):
        return pltpu.make_async_remote_copy(
            src_ref=src, dst_ref=dst, send_sem=ssem, recv_sem=rsem,
            device_id=(to_sec, to_tp), device_id_type=MESH)

    rank_in, rank_out = ib_ref.shape[1], ob_ref.shape[1]

    def prepare_bases():
        gap_in = jnp.zeros((rank_in, width), jnp.float32)
        gap_out = jnp.zeros((EXAMPLES * rank_out, width), jnp.float32)
        for layer in range(2):
            basis_in = ib_ref[layer].astype(jnp.float32)
            basis_out = [ob_ref[layer].astype(jnp.float32)] * EXAMPLES
            ins = [basis_in, gap_in] if layer == 0 else [gap_in, basis_in]
            outs = basis_out + [gap_out] if layer == 0 else [gap_out] + basis_out
            ib_v[layer] = jnp.concatenate(ins, 0).astype(jnp.bfloat16)
            ob_v[layer] = jnp.concatenate(outs, 0).astype(jnp.bfloat16)

    @pl.when(is_top)
    def _():
        @pl.loop(0, micro)
        def _(m):
            for k in range(tp_count):
                top_copy(m, k).start()

    w_copy(1).start()

    @pl.when(has_lower)
    def _():
        w_copy(0).start()

    barrier = pltpu.get_barrier_semaphore()

    def greet(to_sec, to_tp):
        pl.semaphore_signal(barrier, inc=1, device_id=(to_sec, to_tp), device_id_type=MESH)

    for step in range(1, tp_count):
        greet(sec, lax.rem(tp + step, tp_count))

    partner = sec + 1 - 2 * lax.rem(sec, 2)
    for step in range(1, nz):
        greet(partner, peer_z(step))
    for step in range(1, ny):
        greet(partner, peer_y(step))
    for step in range(1, sections):
        greet(lax.rem(sec + step, sections), tp)
    linked = 0
    for when, there in ((far_fed, sec + 1), (far_lower, sec - 1)):
        @pl.when(when)
        def _(there=there):
            for step in range(1, nz):
                greet(there, peer_z(step))
            for step in range(1, ny):
                greet(there, peer_y(step))

        linked = linked + (nz + ny - 2) * when.astype(jnp.int32)
    if helper >= 0:
        for here, there in ((sections - 1, helper), (helper, sections - 1)):
            @pl.when(sec == here)
            def _(there=there):
                for step in range(1, tp_count):
                    greet(there, lax.rem(tp + step, tp_count))

            linked = linked + (tp_count - 1) * (sec == here).astype(jnp.int32)

    def turn_weights(layer):
        w_copy(layer).wait()

        @pl.loop(0, tp_count)
        def _(k):
            columns = pl.ds(pl.multiple_of(k * width, width), width)
            w_t[layer, columns, :] = w_v[layer, :, columns].T

    prepare_bases()
    turn_weights(1)

    @pl.when(jnp.logical_and(has_lower, jnp.logical_not(is_top)))
    def _():
        turn_weights(0)

    pl.semaphore_wait(barrier, tp_count + nz + ny + sections - 4 + linked)

    def slots(buf, m, count, ssem, rsem):
        part = buf.at[m, pl.ds(0, count)]
        return remote(part, part, ssem, rsem, sec, tp)

    def relay_copy(buf, sends, recvs, m, zstep, ystep):
        src = src_at(zstep, 0)
        line = ny - ystep - (0 if zstep else 1)
        return remote(buf.at[m, src], buf.at[m, src], sends.at[m],
                      recvs.at[m, line], sec, peer_y(ystep))

    def forward_copy(buf, sends, recvs, m, ystep):
        src = src_at(0, ystep)
        return remote(buf.at[m, src], buf.at[m, src], sends.at[m],
                      recvs.at[m, ystep], sec, mate * ny + y)

    def spread_copy(buf, sends, recvs, m, zstep):
        return remote(buf.at[m, tp], buf.at[m, tp], sends.at[m], recvs.at[m, 0], sec, peer_z(zstep))

    def lower_own_copy(m):
        return remote(buf_l.at[m], buf_u.at[m, tp], send_l.at[m], recv_x.at[m], sec - 1, tp)

    def lower_z_copy(m, zstep):
        return remote(buf_l.at[m], buf_u.at[m, tp], send_l.at[m], recv_u.at[m, 0],
                      sec - 1, peer_z(zstep))

    def lower_y_copy(m, ystep):
        return remote(buf_l.at[m], buf_u.at[m, tp], send_l.at[m], near_u.at[m, ny - ystep - 1],
                      sec - 1, peer_y(ystep))

    def await_own(m):
        remote(buf_u.at[m, tp], buf_u.at[m, tp], send_my, recv_x.at[m], sec, tp).wait_recv()

    def await_line(buf, recvs, m, ystep):
        slots(buf, m, nz - 1, send_my, recvs.at[m, ystep]).wait_recv()

    def await_near(buf, nears, m, ystep):
        slots(buf, m, 1, send_my, nears.at[m, ystep - 1]).wait_recv()

    def pass_on(buf, sends, recvs, nears, m):
        for ystep in range(1, ny):
            await_near(buf, nears, m, ystep)
            forward_copy(buf, sends, recvs, m, ystep).start()
        await_line(buf, recvs, m, 0)
        for zstep in range(2, nz):
            for ystep in range(1, ny):
                relay_copy(buf, sends, recvs, m, zstep, ystep).start()

    def routed_on(buf, recvs, m, target):
        remote(buf_v.at[m], buf_v.at[m], send_my, recv_v.at[m], sec, tp).wait_recv()
        for zstep in range(nz - 1, 0, -1):
            remote(buf_v.at[m], buf.at[m, tp], send_v.at[m], recvs.at[m, 0],
                   target, src_at(zstep, 0)).start()

    def product(buf, m, layer, ystep, total=None):
        for zstep in range(nz):
            src = src_at(zstep, ystep)
            columns = pl.ds(pl.multiple_of(src * width, width), width)
            term = lax.dot_general(
                buf[m, src], w_t[layer, columns, :], NN, preferred_element_type=jnp.float32)
            total = term if total is None else total + term
        return total

    def upper(m):
        at = pl.ds(pl.multiple_of(m * rows, rows), rows)
        own = buf_u[m, tp]
        floats = own.astype(jnp.float32)
        slope = slope_of(h_ref[1, at, :])
        total = product(buf_u, m, 1, 0)
        for ystep in range(1, ny):
            @pl.when(jnp.logical_not(is_top))
            def _(ystep=ystep):
                await_line(buf_u, recv_u, m, ystep)

            total = product(buf_u, m, 1, ystep, total)
        middle = (floats + slope * total).astype(jnp.bfloat16)
        buf_m[m, tp] = middle

        routed = jnp.logical_and(is_top, top_routed(m))

        @pl.when(jnp.logical_and(has_lower, jnp.logical_not(routed)))
        def _():
            for step in range(1, nz):
                spread_copy(buf_m, send_m, recv_m, m, step).start()

        @pl.when(has_lower)
        def _():
            for step in range(1, ny):
                relay_copy(buf_m, send_m, near_m, m, 0, step).start()

        if helper >= 0:
            @pl.when(routed)
            def _():
                remote(buf_m.at[m, tp], buf_v.at[m], send_m.at[m], recv_v.at[m],
                       helper, tp).start()

        feats = lax.dot_general(
            own, ob_v[1], NT, preferred_element_type=jnp.float32
        ) + lax.dot_general(middle, ob_v[0], NT, preferred_element_type=jnp.float32)
        example = se_ref[m * rows // (micro * rows // se_ref.shape[0])]
        lane_example = lax.rem(
            lax.broadcasted_iota(jnp.int32, feats.shape, 1) // rank_out, EXAMPLES)
        out_v[at, :] = jnp.where(lane_example == example, feats, 0.0)

    def lower(m):
        at = pl.ds(pl.multiple_of(m * rows, rows), rows)
        floats = buf_m[m, tp].astype(jnp.float32)
        slope = slope_of(h_ref[0, at, :])

        total = product(buf_m, m, 0, 0)
        for ystep in range(1, ny):
            await_line(buf_m, recv_m, m, ystep)
            total = product(buf_m, m, 0, ystep, total)
        buf_l[m] = (floats + slope * total).astype(jnp.bfloat16)

        @pl.when(jnp.logical_or(pair_lower, direct(m)))
        def _():
            for step in range(1, nz):
                lower_z_copy(m, step).start()
            for step in range(1, ny):
                lower_y_copy(m, step).start()

        lower_own_copy(m).start()

    def tp_copy(src, dst, ssem, rsem, to_tp):
        return remote(src, dst, ssem, rsem, sec, to_tp)

    others = [(zstep, ystep) for zstep in [*range(nz - 1, 0, -1), 0]
              for ystep in range(ny) if zstep or ystep]

    def share(src_of, dst_ref, ssem, rsem):
        for zstep, ystep in others:
            to = src_at(zstep, ystep)
            tp_copy(src_of(to), dst_ref, ssem, rsem, to).start()

    def shared(buf, ssem, rsem):
        part = buf.at[pl.ds(0, tp_count - 1)]
        return tp_copy(part, part, ssem, rsem, tp)

    def score_copy(step):
        to = lax.rem(sec + step, sections)
        return remote(score_v.at[sec], score_v.at[sec], score_send,
                      score_recv, to, tp)

    def project_inputs():
        part_rows = part_in.shape[1]

        @pl.loop(0, tp_count)
        def _(k):
            at = pl.ds(pl.multiple_of(k * part_rows, part_rows), part_rows)
            total = None
            for layer in range(2):
                floats = h_ref[layer, at, :].astype(jnp.float32)
                activated = (floats * jax.nn.sigmoid(floats)).astype(jnp.bfloat16)
                term = lax.dot_general(
                    activated, ib_v[layer], NT, preferred_element_type=jnp.float32)
                total = term if total is None else total + term
            part_in[k] = total

        share(lambda to: part_in.at[to], got_in.at[tp], part_send, part_recv)
        total = part_in[tp]
        shared(got_in, send_my, part_recv).wait_recv()
        for step in range(1, tp_count):
            total = total + got_in[lax.rem(tp + step, tp_count)]
        full_in[tp] = total
        share(lambda to: full_in.at[tp], full_in.at[tp], full_send, full_recv)

    @pl.when(sec < sections // 2)
    def _():
        project_inputs()

    def spread_upper(m):
        await_own(m)
        for step in range(1, nz):
            spread_copy(buf_u, send_u, recv_u, m, step).start()
        for step in range(1, ny):
            relay_copy(buf_u, send_u, near_u, m, 0, step).start()

    def pass_upper(m):
        @pl.when(jnp.logical_or(pair_upper, direct(m)))
        def _():
            await_own(m)

        pass_on(buf_u, send_u, recv_u, near_u, m)

    def pass_middle(m):
        pass_on(buf_m, send_m, recv_m, near_m, m)

    def within(m):
        return jnp.logical_and(m >= 0, m < micro)

    kind = jnp.where(is_top, 0, jnp.where(far_fed, 2, jnp.where(has_lower, 1, 3)))

    def lag_of(k):
        lag = LAGS[0][k]
        for other in range(1, 4):
            lag = jnp.where(kind == other, LAGS[other][k], lag)
        return lag

    lag_pass, lag_upper, lag_middle, lag_lower = [lag_of(k) for k in range(4)]
    steps = micro + max(max(lags) for lags in LAGS)

    if helper >= 0:
        @pl.when(sec == helper)
        def _():
            @pl.loop(*scaled(TOP_ROUTED))
            def _(m):
                routed_on(buf_m, recv_m, m, sections - 1)

    @pl.loop(0, steps)
    def _(it):
        m_pass = it - lag_pass
        m_up = it - lag_upper
        m_mid = it - lag_middle
        m_low = it - lag_lower

        @pl.when(jnp.logical_and(jnp.logical_and(it < micro, far_fed), jnp.logical_not(direct(it))))
        def _():
            spread_upper(it)

        @pl.when(jnp.logical_and(within(m_pass), jnp.logical_not(is_top)))
        def _():
            pass_upper(m_pass)

        @pl.when(within(m_up))
        def _():
            @pl.when(is_top)
            def _():
                pltpu.make_async_copy(
                    buf_u.at[m_up], buf_u.at[m_up], top_sem.at[m_up]).wait()

            upper(m_up)

        @pl.when(jnp.logical_and(it == 0, is_top))
        def _():
            turn_weights(0)

        @pl.when(jnp.logical_and(within(m_mid), has_lower))
        def _():
            pass_middle(m_mid)

        @pl.when(jnp.logical_and(within(m_low), has_lower))
        def _():
            lower(m_low)

    @pl.when(sec >= sections // 2)
    def _():
        project_inputs()

    shared(full_in, send_my, full_recv).wait_recv()
    lanes = 2 * rank_in
    pairs = EXAMPLES * rank_out
    product_all = lax.dot_general(
        out_v[...], full_in[...].reshape(micro * rows, lanes), (((0,), (0,)), ((), ())),
        precision=lax.Precision.HIGHEST, preferred_element_type=jnp.float32)
    lane = lax.broadcasted_iota(jnp.int32, (pairs, lanes), 1)
    own_grad = jnp.where(lane < rank_in, product_all[:pairs], product_all[pairs:])
    grad_v[tp] = own_grad.astype(jnp.bfloat16)
    share(lambda to: grad_v.at[tp], grad_v.at[tp], grad_send, grad_recv)
    shared(grad_v, send_my, grad_recv).wait_recv()
    total = grad_v[0].astype(jnp.float32)
    for k in range(1, tp_count):
        total = total + grad_v[k].astype(jnp.float32)
    sum_v[...] = total
    half = rank_out // 2
    number = q_ref.shape[1]
    sums = []
    for example in range(EXAMPLES):
        even = sum_v[pl.ds(example * rank_out, half, stride=2), :]
        odd = sum_v[pl.ds(example * rank_out + 1, half, stride=2), :]
        acc = jnp.zeros((number, lanes), jnp.float32)
        for layer in range(2):
            part = slice(layer * rank_in, (layer + 1) * rank_in)
            tiles = jnp.concatenate([even[:, part], odd[:, part]], 1)
            for j in range(half):
                block = q_ref[layer, :, j * lanes:(j + 1) * lanes].astype(jnp.float32)
                acc = acc + tiles[j:j + 1, :] * block
        sums.append(acc)
    score_v[sec] = lax.dot_general(
        jnp.ones((8, lanes), jnp.float32), jnp.concatenate(sums, 0), NT,
        precision=lax.Precision.HIGHEST, preferred_element_type=jnp.float32)
    for step in range(1, sections):
        score_copy(step).start()
    shared(part_in, part_send, send_my).wait_send()
    shared(full_in, full_send, send_my).wait_send()
    shared(grad_v, grad_send, send_my).wait_send()

    def sent(sends, buf, m, count, when):
        @pl.when(when)
        def _():
            slots(buf, m, count, sends.at[m], send_my).wait_send()

    @pl.loop(0, micro)
    def _(m):
        top_far = jnp.logical_and(is_top, top_routed(m))
        spread = jnp.logical_and(far_fed, jnp.logical_not(direct(m)))
        hop = jnp.logical_and(far_lower, jnp.logical_not(direct(m)))
        sent(send_u, buf_u, m, tp_count - 1, spread)
        if ny > 1:
            sent(send_u, buf_u, m, (nz - 1) * (ny - 1),
                 jnp.logical_not(jnp.logical_or(is_top, spread)))
        sent(send_m, buf_m, m, tp_count - 1, jnp.logical_and(has_lower, jnp.logical_not(top_far)))
        sent(send_m, buf_m, m, 1 + nz * (ny - 1), top_far)
        sent(send_l, buf_u, m, nz + ny - 1, jnp.logical_and(has_lower, jnp.logical_not(hop)))
        sent(send_l, buf_u, m, 1, hop)
        if helper >= 0:
            sent(send_v, buf_u, m, nz - 1,
                 jnp.logical_and(sec == helper, top_routed(m)))

    scores = score_v.at[pl.ds(0, sections - 1)]
    remote(scores, scores, send_my, score_recv, sec, tp).wait_recv()
    total = score_v[0]
    for k in range(1, sections):
        total = total + score_v[k]
    for example in range(EXAMPLES):
        score_ref[example:example + 1, :] = total[0:1, example * number:(example + 1) * number]
    remote(scores, scores, score_send, send_my, sec, tp).wait_send()


def shards(
    layer_inputs, weights, input_basis, output_basis, queries, top_cotangent, sequence_example
):
    sections = lax.axis_size("section")
    tp_count = lax.axis_size("tp")
    tokens, width = layer_inputs.shape[1:]
    rows = ROWS
    micro = tokens // rows
    nz, ny = grid_of(tp_count)
    lanes = 2 * input_basis.shape[2]
    pairs = EXAMPLES * output_basis.shape[2]
    number = queries.shape[1]
    dma = pltpu.SemaphoreType.DMA
    vmem = pl.BlockSpec(memory_space=pltpu.VMEM)
    hbm = pl.BlockSpec(memory_space=pl.ANY)
    smem = pl.BlockSpec(memory_space=pltpu.SMEM)
    return pl.pallas_call(
        functools.partial(chain_kernel, sections, tp_count),
        out_shape=jax.ShapeDtypeStruct((EXAMPLES, number), jnp.float32),
        in_specs=[hbm, hbm, vmem, vmem, vmem, vmem, smem],
        out_specs=vmem,
        scratch_shapes=[
            pltpu.VMEM((micro, tp_count, rows, width), jnp.bfloat16),
            pltpu.VMEM((micro, tp_count, rows, width), jnp.bfloat16),
            pltpu.VMEM((micro, rows, width), jnp.bfloat16),
            pltpu.VMEM((micro, rows, width), jnp.bfloat16),
            pltpu.VMEM(weights.shape, jnp.bfloat16),
            pltpu.VMEM((2, weights.shape[2], width), jnp.bfloat16),
            pltpu.VMEM((2, 2 * pairs, width), jnp.bfloat16),
            pltpu.VMEM((2, lanes, width), jnp.bfloat16),
            pltpu.VMEM((tokens, 2 * pairs), jnp.float32),
            pltpu.VMEM((tp_count, tokens // tp_count, lanes), jnp.float32),
            pltpu.VMEM((tp_count, tokens // tp_count, lanes), jnp.float32),
            pltpu.VMEM((tp_count, tokens // tp_count, lanes), jnp.float32),
            pltpu.VMEM((tp_count, pairs, lanes), jnp.bfloat16),
            pltpu.VMEM((pairs, lanes), jnp.float32),
            pltpu.VMEM((sections, 8, EXAMPLES * number), jnp.float32),
            dma((2,)),
            dma((micro,)),
            dma((micro,)),
            dma((micro, ny)),
            dma((micro, ny)),
            dma((micro, max(ny - 1, 1))),
            dma((micro, max(ny - 1, 1))),
            dma((micro,)),
            dma((micro,)),
            dma((micro,)),
            dma((micro,)),
            dma((micro,)),
            dma,
            dma,
            dma,
            dma,
            dma,
            dma,
            dma,
            dma,
            dma,
        ],
        compiler_params=pltpu.CompilerParams(
            collective_id=0, has_side_effects=True, vmem_limit_bytes=56 * 2**20),
    )(
        top_cotangent, weights, layer_inputs, jnp.swapaxes(input_basis, 1, 2),
        jnp.swapaxes(output_basis, 1, 2), queries, sequence_example)


def solution(mesh):
    placed = (
        P("section", None, "tp"),
        P("section", "tp", None),
        P("section", "tp", None),
        P("section", "tp", None),
        P("section", "tp", None),
        P(),
        P(),
    )
    return jax.shard_map(
        shards, mesh=mesh, in_specs=placed, out_specs=P(None, "tp"), check_vma=False
    )
```

```python
import functools

import jax
import jax.numpy as jnp
from jax import lax
from jax.experimental import pallas as pl
from jax.experimental.pallas import tpu as pltpu
from jax.sharding import PartitionSpec as P

EXAMPLES = 2
ROWS = 32
TOP_ROUTED = (6, 14)
DIRECT = (11, 16)
LAGS = ((0, 0, 2, 3), (0, 1, 2, 3), (1, 2, 3, 4), (0, 1, 1, 1))
MESH = pl.DeviceIdType.MESH
NT = (((1,), (1,)), ((), ()))
NN = (((1,), (0,)), ((), ()))


def grid_of(tp_count):
    ny = 1
    while (2 * ny) * (2 * ny) <= tp_count:
        ny *= 2
    return tp_count // ny, ny


def slope_of(hidden):
    floats = hidden.astype(jnp.float32)
    logistic = jax.nn.sigmoid(floats)
    return logistic * (1.0 + floats * (1.0 - logistic))


def chain_kernel(
    sections, tp_count, top_ref, w_ref, h_ref, ib_ref, ob_ref, q_ref, se_ref, score_ref,
    buf_u, buf_m, buf_l, buf_v, w_v, w_t, ob_v, ib_v, out_v, part_in, got_in, full_in, grad_v, sum_v, score_v,
    w_sem, top_sem, recv_x, recv_u, recv_m, near_u, near_m, recv_v, send_u, send_m, send_l, send_v, send_my,
    part_send, part_recv, full_send, full_recv, grad_send, grad_recv, score_send, score_recv,
):
    nz, ny = grid_of(tp_count)
    sec = lax.axis_index("section")
    tp = lax.axis_index("tp")
    z, y = tp // ny, lax.rem(tp, ny)
    micro, _, rows, width = buf_u.shape
    is_top = sec == sections - 1
    has_lower = sec > 0
    pair_lower = lax.rem(sec, 2) == 1
    pair_upper = jnp.logical_not(pair_lower)
    helper = sections - 4

    def scaled(span):
        return [part * micro // 16 for part in span]

    def in_span(m, span):
        low, high = scaled(span)
        return jnp.logical_and(m >= low, m < high)

    def top_routed(m):
        return in_span(m, TOP_ROUTED if helper >= 0 else (0, 0))

    def direct(m):
        return in_span(m, DIRECT)

    far_fed = jnp.logical_and(pair_lower, jnp.logical_not(is_top))
    far_lower = jnp.logical_and(pair_upper, has_lower)

    far = [z]
    for k in range(nz - 1):
        down = nz - 1 - k
        from_low = down - (z >= down).astype(jnp.int32)
        from_high = k + (z <= k).astype(jnp.int32)
        far.append(jnp.where(z < nz // 2, from_low, from_high))
    near = far[:1] + far[:0:-1]
    mate = z + 1 - 2 * lax.rem(z, 2)

    def peer_z(step):
        return far[step] * ny + y

    def peer_y(step):
        return z * ny + lax.rem(y + step, ny)

    def src_at(zstep, ystep):
        return near[zstep] * ny + lax.rem(y + ystep, ny)

    def w_copy(layer):
        return pltpu.make_async_copy(w_ref.at[layer], w_v.at[layer], w_sem.at[layer])

    def top_copy(m, k):
        return pltpu.make_async_copy(
            top_ref.at[pl.ds(pl.multiple_of(m * rows, rows), rows), pl.ds(k * width, width)],
            buf_u.at[m, k], top_sem.at[m])

    def remote(src, dst, ssem, rsem, to_sec, to_tp):
        return pltpu.make_async_remote_copy(
            src_ref=src, dst_ref=dst, send_sem=ssem, recv_sem=rsem,
            device_id=(to_sec, to_tp), device_id_type=MESH)

    rank_in, rank_out = ib_ref.shape[1], ob_ref.shape[1]

    def prepare_bases():
        gap_in = jnp.zeros((rank_in, width), jnp.float32)
        gap_out = jnp.zeros((EXAMPLES * rank_out, width), jnp.float32)
        for layer in range(2):
            basis_in = ib_ref[layer].astype(jnp.float32)
            basis_out = [ob_ref[layer].astype(jnp.float32)] * EXAMPLES
            ins = [basis_in, gap_in] if layer == 0 else [gap_in, basis_in]
            outs = basis_out + [gap_out] if layer == 0 else [gap_out] + basis_out
            ib_v[layer] = jnp.concatenate(ins, 0).astype(jnp.bfloat16)
            ob_v[layer] = jnp.concatenate(outs, 0).astype(jnp.bfloat16)

    @pl.when(is_top)
    def _():
        @pl.loop(0, micro)
        def _(m):
            for k in range(tp_count):
                top_copy(m, k).start()

    w_copy(1).start()

    @pl.when(has_lower)
    def _():
        w_copy(0).start()

    barrier = pltpu.get_barrier_semaphore()

    def greet(to_sec, to_tp):
        pl.semaphore_signal(barrier, inc=1, device_id=(to_sec, to_tp), device_id_type=MESH)

    for step in range(1, tp_count):
        greet(sec, lax.rem(tp + step, tp_count))

    partner = sec + 1 - 2 * lax.rem(sec, 2)
    for step in range(1, nz):
        greet(partner, peer_z(step))
    for step in range(1, ny):
        greet(partner, peer_y(step))
    for step in range(1, sections):
        greet(lax.rem(sec + step, sections), tp)
    linked = 0
    for when, there in ((far_fed, sec + 1), (far_lower, sec - 1)):
        @pl.when(when)
        def _(there=there):
            for step in range(1, nz):
                greet(there, peer_z(step))
            for step in range(1, ny):
                greet(there, peer_y(step))

        linked = linked + (nz + ny - 2) * when.astype(jnp.int32)
    if helper >= 0:
        for here, there in ((sections - 1, helper), (helper, sections - 1)):
            @pl.when(sec == here)
            def _(there=there):
                for step in range(1, tp_count):
                    greet(there, lax.rem(tp + step, tp_count))

            linked = linked + (tp_count - 1) * (sec == here).astype(jnp.int32)

    def turn_weights(layer):
        w_copy(layer).wait()

        @pl.loop(0, tp_count)
        def _(k):
            columns = pl.ds(pl.multiple_of(k * width, width), width)
            w_t[layer, columns, :] = w_v[layer, :, columns].T

    prepare_bases()
    turn_weights(1)

    @pl.when(jnp.logical_and(has_lower, jnp.logical_not(is_top)))
    def _():
        turn_weights(0)

    pl.semaphore_wait(barrier, tp_count + nz + ny + sections - 4 + linked)

    def slots(buf, m, count, ssem, rsem):
        part = buf.at[m, pl.ds(0, count)]
        return remote(part, part, ssem, rsem, sec, tp)

    def relay_copy(buf, sends, recvs, m, zstep, ystep):
        src = src_at(zstep, 0)
        line = ny - ystep - (0 if zstep else 1)
        return remote(buf.at[m, src], buf.at[m, src], sends.at[m],
                      recvs.at[m, line], sec, peer_y(ystep))

    def forward_copy(buf, sends, recvs, m, ystep):
        src = src_at(0, ystep)
        return remote(buf.at[m, src], buf.at[m, src], sends.at[m],
                      recvs.at[m, ystep], sec, mate * ny + y)

    def spread_copy(buf, sends, recvs, m, zstep):
        return remote(buf.at[m, tp], buf.at[m, tp], sends.at[m], recvs.at[m, 0], sec, peer_z(zstep))

    def lower_own_copy(m):
        return remote(buf_l.at[m], buf_u.at[m, tp], send_l.at[m], recv_x.at[m], sec - 1, tp)

    def lower_z_copy(m, zstep):
        return remote(buf_l.at[m], buf_u.at[m, tp], send_l.at[m], recv_u.at[m, 0],
                      sec - 1, peer_z(zstep))

    def lower_y_copy(m, ystep):
        return remote(buf_l.at[m], buf_u.at[m, tp], send_l.at[m], near_u.at[m, ny - ystep - 1],
                      sec - 1, peer_y(ystep))

    def await_own(m):
        remote(buf_u.at[m, tp], buf_u.at[m, tp], send_my, recv_x.at[m], sec, tp).wait_recv()

    def await_line(buf, recvs, m, ystep):
        slots(buf, m, nz - 1, send_my, recvs.at[m, ystep]).wait_recv()

    def await_near(buf, nears, m, ystep):
        slots(buf, m, 1, send_my, nears.at[m, ystep - 1]).wait_recv()

    def pass_on(buf, sends, recvs, nears, m):
        for ystep in range(1, ny):
            await_near(buf, nears, m, ystep)
            forward_copy(buf, sends, recvs, m, ystep).start()
        await_line(buf, recvs, m, 0)
        for zstep in range(2, nz):
            for ystep in range(1, ny):
                relay_copy(buf, sends, recvs, m, zstep, ystep).start()

    def routed_on(buf, recvs, m, target):
        remote(buf_v.at[m], buf_v.at[m], send_my, recv_v.at[m], sec, tp).wait_recv()
        for zstep in range(nz - 1, 0, -1):
            remote(buf_v.at[m], buf.at[m, tp], send_v.at[m], recvs.at[m, 0],
                   target, src_at(zstep, 0)).start()

    def product(buf, m, layer, ystep, total=None):
        for zstep in range(nz):
            src = src_at(zstep, ystep)
            columns = pl.ds(pl.multiple_of(src * width, width), width)
            term = lax.dot_general(
                buf[m, src], w_t[layer, columns, :], NN, preferred_element_type=jnp.float32)
            total = term if total is None else total + term
        return total

    def upper(m):
        at = pl.ds(pl.multiple_of(m * rows, rows), rows)
        own = buf_u[m, tp]
        floats = own.astype(jnp.float32)
        slope = slope_of(h_ref[1, at, :])
        total = product(buf_u, m, 1, 0)
        for ystep in range(1, ny):
            @pl.when(jnp.logical_not(is_top))
            def _(ystep=ystep):
                await_line(buf_u, recv_u, m, ystep)

            total = product(buf_u, m, 1, ystep, total)
        middle = (floats + slope * total).astype(jnp.bfloat16)
        buf_m[m, tp] = middle

        routed = jnp.logical_and(is_top, top_routed(m))

        @pl.when(jnp.logical_and(has_lower, jnp.logical_not(routed)))
        def _():
            for step in range(1, nz):
                spread_copy(buf_m, send_m, recv_m, m, step).start()

        @pl.when(has_lower)
        def _():
            for step in range(1, ny):
                relay_copy(buf_m, send_m, near_m, m, 0, step).start()

        if helper >= 0:
            @pl.when(routed)
            def _():
                remote(buf_m.at[m, tp], buf_v.at[m], send_m.at[m], recv_v.at[m],
                       helper, tp).start()

        feats = lax.dot_general(
            own, ob_v[1], NT, preferred_element_type=jnp.float32
        ) + lax.dot_general(middle, ob_v[0], NT, preferred_element_type=jnp.float32)
        example = se_ref[m * rows // (micro * rows // se_ref.shape[0])]
        lane_example = lax.rem(
            lax.broadcasted_iota(jnp.int32, feats.shape, 1) // rank_out, EXAMPLES)
        out_v[at, :] = jnp.where(lane_example == example, feats, 0.0)

    def lower(m):
        at = pl.ds(pl.multiple_of(m * rows, rows), rows)
        floats = buf_m[m, tp].astype(jnp.float32)
        slope = slope_of(h_ref[0, at, :])

        total = product(buf_m, m, 0, 0)
        for ystep in range(1, ny):
            await_line(buf_m, recv_m, m, ystep)
            total = product(buf_m, m, 0, ystep, total)
        buf_l[m] = (floats + slope * total).astype(jnp.bfloat16)

        @pl.when(jnp.logical_or(pair_lower, direct(m)))
        def _():
            for step in range(1, nz):
                lower_z_copy(m, step).start()
            for step in range(1, ny):
                lower_y_copy(m, step).start()

        lower_own_copy(m).start()

    def tp_copy(src, dst, ssem, rsem, to_tp):
        return remote(src, dst, ssem, rsem, sec, to_tp)

    others = [(zstep, ystep) for zstep in [*range(nz - 1, 0, -1), 0]
              for ystep in range(ny) if zstep or ystep]

    def share(src_of, dst_ref, ssem, rsem):
        for zstep, ystep in others:
            to = src_at(zstep, ystep)
            tp_copy(src_of(to), dst_ref, ssem, rsem, to).start()

    def shared(buf, ssem, rsem):
        part = buf.at[pl.ds(0, tp_count - 1)]
        return tp_copy(part, part, ssem, rsem, tp)

    def score_copy(step):
        to = lax.rem(sec + step, sections)
        return remote(score_v.at[sec], score_v.at[sec], score_send,
                      score_recv, to, tp)

    def project_inputs():
        part_rows = part_in.shape[1]

        @pl.loop(0, tp_count)
        def _(k):
            at = pl.ds(pl.multiple_of(k * part_rows, part_rows), part_rows)
            total = None
            for layer in range(2):
                floats = h_ref[layer, at, :].astype(jnp.float32)
                activated = (floats * jax.nn.sigmoid(floats)).astype(jnp.bfloat16)
                term = lax.dot_general(
                    activated, ib_v[layer], NT, preferred_element_type=jnp.float32)
                total = term if total is None else total + term
            part_in[k] = total

        share(lambda to: part_in.at[to], got_in.at[tp], part_send, part_recv)
        total = part_in[tp]
        shared(got_in, send_my, part_recv).wait_recv()
        for step in range(1, tp_count):
            total = total + got_in[lax.rem(tp + step, tp_count)]
        full_in[tp] = total
        share(lambda to: full_in.at[tp], full_in.at[tp], full_send, full_recv)

    @pl.when(sec < sections // 2)
    def _():
        project_inputs()

    def spread_upper(m):
        await_own(m)
        for step in range(1, nz):
            spread_copy(buf_u, send_u, recv_u, m, step).start()
        for step in range(1, ny):
            relay_copy(buf_u, send_u, near_u, m, 0, step).start()

    def pass_upper(m):
        @pl.when(jnp.logical_or(pair_upper, direct(m)))
        def _():
            await_own(m)

        pass_on(buf_u, send_u, recv_u, near_u, m)

    def pass_middle(m):
        pass_on(buf_m, send_m, recv_m, near_m, m)

    def within(m):
        return jnp.logical_and(m >= 0, m < micro)

    kind = jnp.where(is_top, 0, jnp.where(far_fed, 2, jnp.where(has_lower, 1, 3)))

    def lag_of(k):
        lag = LAGS[0][k]
        for other in range(1, 4):
            lag = jnp.where(kind == other, LAGS[other][k], lag)
        return lag

    lag_pass, lag_upper, lag_middle, lag_lower = [lag_of(k) for k in range(4)]
    steps = micro + max(max(lags) for lags in LAGS)

    if helper >= 0:
        @pl.when(sec == helper)
        def _():
            @pl.loop(*scaled(TOP_ROUTED))
            def _(m):
                routed_on(buf_m, recv_m, m, sections - 1)

    @pl.loop(0, steps)
    def _(it):
        m_pass = it - lag_pass
        m_up = it - lag_upper
        m_mid = it - lag_middle
        m_low = it - lag_lower

        @pl.when(jnp.logical_and(jnp.logical_and(it < micro, far_fed), jnp.logical_not(direct(it))))
        def _():
            spread_upper(it)

        @pl.when(jnp.logical_and(within(m_pass), jnp.logical_not(is_top)))
        def _():
            pass_upper(m_pass)

        @pl.when(within(m_up))
        def _():
            @pl.when(is_top)
            def _():
                pltpu.make_async_copy(
                    buf_u.at[m_up], buf_u.at[m_up], top_sem.at[m_up]).wait()

            upper(m_up)

        @pl.when(jnp.logical_and(it == 0, is_top))
        def _():
            turn_weights(0)

        @pl.when(jnp.logical_and(within(m_mid), has_lower))
        def _():
            pass_middle(m_mid)

        @pl.when(jnp.logical_and(within(m_low), has_lower))
        def _():
            lower(m_low)

    @pl.when(sec >= sections // 2)
    def _():
        project_inputs()

    shared(full_in, send_my, full_recv).wait_recv()
    lanes = 2 * rank_in
    pairs = EXAMPLES * rank_out
    product_all = lax.dot_general(
        out_v[...], full_in[...].reshape(micro * rows, lanes), (((0,), (0,)), ((), ())),
        precision=lax.Precision.HIGHEST, preferred_element_type=jnp.float32)
    lane = lax.broadcasted_iota(jnp.int32, (pairs, lanes), 1)
    own_grad = jnp.where(lane < rank_in, product_all[:pairs], product_all[pairs:])
    grad_v[tp] = own_grad.astype(jnp.bfloat16)
    share(lambda to: grad_v.at[tp], grad_v.at[tp], grad_send, grad_recv)
    shared(grad_v, send_my, grad_recv).wait_recv()
    total = grad_v[0].astype(jnp.float32)
    for k in range(1, tp_count):
        total = total + grad_v[k].astype(jnp.float32)
    sum_v[...] = total
    half = rank_out // 2
    number = q_ref.shape[1]
    sums = []
    for example in range(EXAMPLES):
        even = sum_v[pl.ds(example * rank_out, half, stride=2), :]
        odd = sum_v[pl.ds(example * rank_out + 1, half, stride=2), :]
        acc = jnp.zeros((number, lanes), jnp.float32)
        for layer in range(2):
            part = slice(layer * rank_in, (layer + 1) * rank_in)
            tiles = jnp.concatenate([even[:, part], odd[:, part]], 1)
            for j in range(half):
                block = q_ref[layer, :, j * lanes:(j + 1) * lanes].astype(jnp.float32)
                acc = acc + tiles[j:j + 1, :] * block
        sums.append(acc)
    score_v[sec] = lax.dot_general(
        jnp.ones((8, lanes), jnp.float32), jnp.concatenate(sums, 0), NT,
        precision=lax.Precision.HIGHEST, preferred_element_type=jnp.float32)
    for step in range(1, sections):
        score_copy(step).start()
    shared(part_in, part_send, send_my).wait_send()
    shared(full_in, full_send, send_my).wait_send()
    shared(grad_v, grad_send, send_my).wait_send()

    def sent(sends, buf, m, count, when):
        @pl.when(when)
        def _():
            slots(buf, m, count, sends.at[m], send_my).wait_send()

    @pl.loop(0, micro)
    def _(m):
        top_far = jnp.logical_and(is_top, top_routed(m))
        spread = jnp.logical_and(far_fed, jnp.logical_not(direct(m)))
        hop = jnp.logical_and(far_lower, jnp.logical_not(direct(m)))
        sent(send_u, buf_u, m, tp_count - 1, spread)
        if ny > 1:
            sent(send_u, buf_u, m, (nz - 1) * (ny - 1),
                 jnp.logical_not(jnp.logical_or(is_top, spread)))
        sent(send_m, buf_m, m, tp_count - 1, jnp.logical_and(has_lower, jnp.logical_not(top_far)))
        sent(send_m, buf_m, m, 1 + nz * (ny - 1), top_far)
        sent(send_l, buf_u, m, nz + ny - 1, jnp.logical_and(has_lower, jnp.logical_not(hop)))
        sent(send_l, buf_u, m, 1, hop)
        if helper >= 0:
            sent(send_v, buf_u, m, nz - 1,
                 jnp.logical_and(sec == helper, top_routed(m)))

    scores = score_v.at[pl.ds(0, sections - 1)]
    remote(scores, scores, send_my, score_recv, sec, tp).wait_recv()
    total = score_v[0]
    for k in range(1, sections):
        total = total + score_v[k]
    for example in range(EXAMPLES):
        score_ref[example:example + 1, :] = total[0:1, example * number:(example + 1) * number]
    remote(scores, scores, score_send, send_my, sec, tp).wait_send()


def shards(
    layer_inputs, weights, input_basis, output_basis, queries, top_cotangent, sequence_example
):
    sections = lax.axis_size("section")
    tp_count = lax.axis_size("tp")
    tokens, width = layer_inputs.shape[1:]
    rows = ROWS
    micro = tokens // rows
    nz, ny = grid_of(tp_count)
    lanes = 2 * input_basis.shape[2]
    pairs = EXAMPLES * output_basis.shape[2]
    number = queries.shape[1]
    dma = pltpu.SemaphoreType.DMA
    vmem = pl.BlockSpec(memory_space=pltpu.VMEM)
    hbm = pl.BlockSpec(memory_space=pl.ANY)
    smem = pl.BlockSpec(memory_space=pltpu.SMEM)
    return pl.pallas_call(
        functools.partial(chain_kernel, sections, tp_count),
        out_shape=jax.ShapeDtypeStruct((EXAMPLES, number), jnp.float32),
        in_specs=[hbm, hbm, vmem, vmem, vmem, vmem, smem],
        out_specs=vmem,
        scratch_shapes=[
            pltpu.VMEM((micro, tp_count, rows, width), jnp.bfloat16),
            pltpu.VMEM((micro, tp_count, rows, width), jnp.bfloat16),
            pltpu.VMEM((micro, rows, width), jnp.bfloat16),
            pltpu.VMEM((micro, rows, width), jnp.bfloat16),
            pltpu.VMEM(weights.shape, jnp.bfloat16),
            pltpu.VMEM((2, weights.shape[2], width), jnp.bfloat16),
            pltpu.VMEM((2, 2 * pairs, width), jnp.bfloat16),
            pltpu.VMEM((2, lanes, width), jnp.bfloat16),
            pltpu.VMEM((tokens, 2 * pairs), jnp.float32),
            pltpu.VMEM((tp_count, tokens // tp_count, lanes), jnp.float32),
            pltpu.VMEM((tp_count, tokens // tp_count, lanes), jnp.float32),
            pltpu.VMEM((tp_count, tokens // tp_count, lanes), jnp.float32),
            pltpu.VMEM((tp_count, pairs, lanes), jnp.bfloat16),
            pltpu.VMEM((pairs, lanes), jnp.float32),
            pltpu.VMEM((sections, 8, EXAMPLES * number), jnp.float32),
            dma((2,)),
            dma((micro,)),
            dma((micro,)),
            dma((micro, ny)),
            dma((micro, ny)),
            dma((micro, max(ny - 1, 1))),
            dma((micro, max(ny - 1, 1))),
            dma((micro,)),
            dma((micro,)),
            dma((micro,)),
            dma((micro,)),
            dma((micro,)),
            dma,
            dma,
            dma,
            dma,
            dma,
            dma,
            dma,
            dma,
            dma,
        ],
        compiler_params=pltpu.CompilerParams(
            collective_id=0, has_side_effects=True, vmem_limit_bytes=56 * 2**20),
    )(
        top_cotangent, weights, layer_inputs, jnp.swapaxes(input_basis, 1, 2),
        jnp.swapaxes(output_basis, 1, 2), queries, sequence_example)


def solution(mesh):
    placed = (
        P("section", None, "tp"),
        P("section", "tp", None),
        P("section", "tp", None),
        P("section", "tp", None),
        P("section", "tp", None),
        P(),
        P(),
    )
    return jax.shard_map(
        shards, mesh=mesh, in_specs=placed, out_specs=P(None, "tp"), check_vma=False
    )
```
